32 devices in a mesh: groups: 2 (over x), corpus: 16 (over z, y, core).
Axes of the slice: x: 2, y: 2, z: 4, core: 2. Of those that a mesh axis runs over, the one named last changes fastest.
Arguments:
- queries: bfloat16 [1792, 32, 128], P(('groups', 'corpus')), parts along dimension 0, may hold values from -6 to 6
- passages: bfloat16 [4096, 128, 128], P(('groups', 'corpus')), parts along dimension 0, may hold values from -0.5 to 0.5
- lengths: int32 [4096], P(('groups', 'corpus')), parts along dimension 0, may hold values from 8 to 128
- candidates: int32 [32, 128], P(('groups', 'corpus')), parts along dimension 0, may hold values from 0 to 2047, as said below
Outputs:
- scores: float32 [1792, 128], P(('groups', 'corpus')), parts along dimension 0
- best_scores: float32 [1792, 100], P(('groups', 'corpus')), parts along dimension 0
The draws below stay inside these ranges and needn't reach their ends.
There are 2 independent parts, one for each index of `groups`. The reference program is written for one: setup_inputs(seed, part) draws one part's arguments, and reference() takes and returns one part's arrays. A program takes and returns all parts, laid end to end along the dimension named above; each array names one. Nothing has to cross between parts.
Inputs may be any that keep to these rules, and one draw needn't show every extreme that they name: Row b lists the candidates of queries b * 56 to (b + 1) * 56 - 1. Passage p is held by owner p // 128. In every row at most 12 entries share an owner, and in every row some owner holds exactly 12 of them. Entries may repeat. `lengths`: rows of a tile at or past its length are padding.
All inputs are finite; a program needn't handle non-finite values.
Results may differ from the reference program's by a relative error of at most 0.0003.
Values may be sent and summed in bfloat16 or wider, within the bound.
A program may use at most 128 MiB of HBM per device.

```python
import jax
import jax.numpy as jnp
from jax import lax

D = 128
QTOK = 32
PTOK = 128
CAND = 128
TOPK = 100
Q_DEV = 56
P_DEV = 128
BLOCKS = 16
CAP = 12
QUERIES = 896
PASSAGES = 2048


def draw_candidates(key, part):
    subkeys = jax.random.split(key, 5)
    all_slots = BLOCKS * CAP
    popular = (jax.random.randint(subkeys[0], (BLOCKS,), 0, 8) == 0).astype(jnp.int32)
    leader = jax.random.randint(subkeys[1], (), 0, BLOCKS)
    levels = jnp.where(jnp.arange(BLOCKS) == leader, 2, popular)
    jitter = jax.random.randint(subkeys[2], (BLOCKS, BLOCKS, CAP), 0, 65536)
    slot_score = (jitter + levels[None, :, None] * 65536).reshape(BLOCKS, all_slots)
    slot_score = slot_score * all_slots + jnp.arange(all_slots, dtype=jnp.int32)[None, :]
    picked = lax.top_k(slot_score, CAND)[1]
    owner_of = picked // CAP
    local_id = jax.random.randint(subkeys[3], (BLOCKS, CAND), 0, P_DEV)
    passage_ids = owner_of * P_DEV + local_id
    shuffle_score = jax.random.randint(subkeys[4], (BLOCKS, CAND), 0, 65536) * CAND + jnp.arange(CAND, dtype=jnp.int32)[None, :]
    position = jnp.argsort(shuffle_score, axis=1, stable=True)
    return jnp.take_along_axis(passage_ids, position, axis=1).astype(jnp.int32)


def set_ends(drawn, key, low, top_value):
    index_at = [jax.random.randint(jax.random.fold_in(key, axis), (), 0, length) for axis, length in enumerate(drawn.shape)]
    main_axis = drawn.shape.index(max(drawn.shape))
    neighbour = index_at[:main_axis] + [(index_at[main_axis] + 1) % drawn.shape[main_axis]] + index_at[main_axis + 1:]
    return drawn.at[tuple(index_at)].set(low).at[tuple(neighbour)].set(top_value)


def block_scale(own_key, shape, pieces, least, high):
    loudness = 1.0
    for axis_at, parts in pieces:
        steps = jax.random.uniform(jax.random.fold_in(jax.random.fold_in(own_key, 6), axis_at), (parts,), jnp.float32, least / len(pieces), high / len(pieces))
        loudness = loudness * jnp.repeat(jnp.exp(steps), shape[axis_at] // parts).reshape((-1,) + (1,) * (len(shape) - 1 - axis_at))
    return loudness


def scatter_about(own_key, shape, scale, limit, cuts=(), held_as=jnp.bfloat16):
    result = jax.random.normal(own_key, shape, jnp.float32) * scale
    if len(cuts) > 0:
        result = block_scale(own_key, shape, cuts, -0.22, 0.18) * result
    return jnp.clip(result, min=-limit, max=limit).astype(held_as)


def setup_inputs(seed: int = 0, part: int = 0) -> dict:
    key_list = jax.random.split(jax.random.key(seed), 5)
    part_splits = jax.random.split(jax.random.fold_in(key_list[4], part), 5)
    return {
        "queries": scatter_about(part_splits[0], (QUERIES, QTOK, D), 1.0, 6.0, ((0, 16),)),
        "passages": scatter_about(part_splits[1], (PASSAGES, PTOK, D), D ** -0.5, 0.5, ((0, 16),)),
        "lengths": set_ends(jax.random.randint(part_splits[2], (PASSAGES,), max(1, PTOK // 16), PTOK + 1), jax.random.fold_in(part_splits[2], 1), max(1, PTOK // 16), PTOK).astype(jnp.int32),
        "candidates": draw_candidates(jax.random.fold_in(jax.random.fold_in(key_list[4], part), 71), part),
    }


def reference(queries, passages, lengths, candidates):
    def one_block(block_idx):
        query_rows = lax.dynamic_slice_in_dim(queries, block_idx * Q_DEV, Q_DEV, 0)
        query_rows = query_rows.reshape(Q_DEV * QTOK, D).astype(jnp.float32)
        passage_ids = candidates[block_idx]
        tile_set = passages[passage_ids]
        tile_len = lengths[passage_ids]
        inside = lax.broadcasted_iota(jnp.int32, (CAND, PTOK), 1) < tile_len[:, None]
        tile_set = jnp.where(inside[:, :, None], tile_set, tile_set[:, :1, :]).astype(jnp.float32)
        similar = jnp.einsum('rd,cpd->rcp', query_rows, tile_set)
        nearest = jnp.max(similar, axis=2)
        return jnp.sum(nearest.reshape(Q_DEV, QTOK, CAND), axis=1) / float(QTOK)

    scores = lax.map(one_block, jnp.arange(BLOCKS, dtype=jnp.int32)).reshape(QUERIES, CAND)
    best_scores = lax.top_k(scores, TOPK)[0]
    return scores, best_scores
```

```python
import functools

import jax
import jax.numpy as jnp
from jax import lax
from jax.experimental import pallas as pl
from jax.experimental.pallas import tpu as pltpu
from jax.sharding import PartitionSpec as P

TOPK = 100
MESH = pl.DeviceIdType.MESH


def pick_tile(rows, tok):
    tile = 256
    while rows % tile or tile % tok:
        tile //= 2
    return tile


def sort_down(x):
    count, width = x.shape
    index = lax.broadcasted_iota(jnp.int32, (count // 8, 8, width), 0) * 8
    index = index + lax.broadcasted_iota(jnp.int32, (count // 8, 8, width), 1)
    x = x.reshape(count // 8, 8, width)
    size = 2
    while size <= count:
        gap = size // 2
        falling = (index // size) % 2 == 0
        while gap >= 1:
            low = (index // gap) % 2 == 0
            if gap >= 8:
                hop = gap // 8
                y = x.reshape(count // (2 * gap), 2, hop, 8, width)
                y = jnp.concatenate([y[:, 1:], y[:, :1]], axis=1)
                other = y.reshape(x.shape)
            else:
                other = jnp.where(low, pltpu.roll(x, 8 - gap, 1), pltpu.roll(x, gap, 1))
            x = jnp.where(low == falling, jnp.maximum(x, other), jnp.minimum(x, other))
            gap //= 2
        size *= 2
    return x.reshape(count, width)


def split3(x):
    high = x.astype(jnp.bfloat16)
    rest = x - high.astype(jnp.float32)
    mid = rest.astype(jnp.bfloat16)
    low = (rest - mid.astype(jnp.float32)).astype(jnp.bfloat16)
    return high, mid, low


def kernel(cfg, cand_hbm, len_hbm, q_hbm, p_hbm, out_ref, place_ref, qall, pas, cand_v, len_s,
           table, wanted, place, fold, stage, send_buf, got, q_send, q_recv, sib_send, sib_recv,
           end_send, end_recv, near_send, near_recv, tail_send, tail_recv, t_send, t_recv,
           tsib_send, tsib_recv, sm_sem, sc_send, sc_recv, loc_sem):
    n, ways, cap, per_owner, tile_rows, rows, feature, tok, col = cfg
    chips = n // 2
    half = chips // 2
    depth = chips // ways
    units = rows // col
    cut = (units + 1) // 2
    spans = []
    for lo, hi in ((0, cut), (cut, units)):
        mid = (lo + hi + 1) // 2
        spans += [(a, b) for a, b in ((lo, mid), (mid, hi)) if b > a]
    pieces = len(spans)
    slots = send_buf.shape[1]
    number = cand_hbm.shape[1]
    me = lax.axis_index("corpus")
    core = lax.rem(me, 2)
    chip = me // 2
    if ways == 2:
        zz, yy = chip // 2, lax.rem(chip, 2)
        pos = (1 - yy) * zz + yy * (2 * depth - 1 - zz)
    else:
        pos = chip

    def at(p, c):
        p = lax.rem(p + 2 * chips, chips)
        if ways == 2:
            far = p // depth
            p = (1 - far) * (2 * p) + far * ((2 * depth - 1 - p) * 2 + 1)
        return p * 2 + c

    sib = at(pos, 1 - core)
    toward = (at(pos + 1, core), at(pos - 1, core))

    def origin(d, s, c):
        return at(pos - s if d == 0 else pos + s, c)

    def remote(src, dst, send, recv, peer):
        return pltpu.make_async_remote_copy(
            src_ref=src, dst_ref=dst, send_sem=send, recv_sem=recv,
            device_id={"corpus": peer}, device_id_type=MESH)

    def span_of(lo, hi):
        return pl.ds(lo * col, (hi - lo) * col)

    def first(d, k):
        cut_k = span_of(*spans[k])
        return remote(q_hbm.at[cut_k, :], qall.at[me, cut_k, :],
                      q_send.at[d, 1, k], q_recv.at[d, 1, k], toward[d])

    def hop(d, s, k, b):
        piece = qall.at[b, span_of(*spans[k]), :]
        return remote(piece, piece, q_send.at[d, s, k], q_recv.at[d, s, k], toward[d])

    def share(d, s, k, b):
        piece = qall.at[b, span_of(*spans[k]), :]
        return remote(piece, piece, sib_send.at[d, s, k], sib_recv.at[d, s, k], sib)

    def near_out(k):
        cut_k = span_of(*spans[k])
        return remote(q_hbm.at[cut_k, :], qall.at[me, cut_k, :],
                      near_send.at[k], near_recv.at[k], sib)

    def near_in(k):
        piece = qall.at[sib, span_of(*spans[k]), :]
        return remote(piece, piece, near_send.at[k], near_recv.at[k], sib)

    def end_hop(e, u, b):
        d = lax.rem(e + core, 2)
        piece = qall.at[b, span_of(u, u + 1), :]
        return remote(piece, piece, end_send.at[u], end_recv.at[u], at(pos + 1 - 2 * d, core))

    def end_share(u, b):
        piece = qall.at[b, span_of(u, u + 1), :]
        return remote(piece, piece, tail_send.at[u], tail_recv.at[u], sib)

    def table_hop(d, s, b):
        return remote(table.at[d, b], table.at[d, b], t_send.at[d, s], t_recv.at[d, s], toward[d])

    def table_share(d, s, b):
        return remote(table.at[d, b], table.at[d, b], tsib_send.at[d, s], tsib_recv.at[d, s], sib)

    my_row = me * slots // 128
    my_lane = lax.rem(me * slots, 128)

    def to_scalar(d, b, who):
        return pltpu.make_async_copy(table.at[d, b, pl.ds(my_row, 1), :],
                                     wanted.at[d, pl.ds(b, 1), :], sm_sem.at[who, d])

    def score_copy(b):
        return remote(send_buf.at[b], got.at[me], sc_send.at[b], sc_recv.at[me], b)

    def score_in(b):
        return remote(send_buf.at[b], got.at[b], sc_send.at[b], sc_recv.at[b], b)

    barrier = pltpu.get_barrier_semaphore()
    for peer in (*toward, sib):
        pl.semaphore_signal(barrier, inc=1, device_id={"corpus": peer}, device_id_type=MESH)
    c_load = pltpu.make_async_copy(cand_hbm, cand_v, loc_sem.at[0])
    q_load = pltpu.make_async_copy(q_hbm, qall.at[me], loc_sem.at[1])
    p_load = pltpu.make_async_copy(p_hbm, pas, loc_sem.at[2])
    l_load = pltpu.make_async_copy(len_hbm, len_s, loc_sem.at[3])
    c_load.start()
    l_load.start()
    p_load.start()
    q_load.start()
    pl.semaphore_wait(barrier, 3)
    for d in range(2):
        first(d, 0).start()

    c_load.wait()
    across = jnp.broadcast_to(cand_v[...], (number, number))
    down = across.T
    down_owner = lax.div(down, per_owner)
    local_id = down[:, :1] - down_owner[:, :1] * per_owner
    r_at = lax.broadcasted_iota(jnp.int32, (number, number), 0)
    c_at = lax.broadcasted_iota(jnp.int32, (number, number), 1)
    ahead = jnp.where((lax.div(across, per_owner) == down_owner) & (c_at < r_at), 1.0, 0.0)
    slot = down_owner[:, :1].astype(jnp.float32) * float(slots) + jnp.sum(ahead, axis=1, keepdims=True)
    slot_at = lax.broadcasted_iota(jnp.int32, place.shape, 1).astype(jnp.float32)
    spot = slot_at == slot
    line = jnp.max(jnp.where(spot, local_id, 0), axis=0, keepdims=True)
    line = jnp.concatenate([line[:, i * 128:(i + 1) * 128] for i in range(n * slots // 128)], axis=0)
    for d in range(2):
        table[d, me] = line
    place[...] = jnp.where(spot, 1.0, 0.0).astype(place.dtype)
    row_at = lax.broadcasted_iota(jnp.int32, (col, 128), 0) // tok
    lane_at = lax.broadcasted_iota(jnp.int32, (col, 128), 1)
    fold[...] = jnp.where(row_at == lane_at, 1.0, 0.0).astype(fold.dtype)
    for d in range(2):
        table_hop(d, 1, me).start()
    table_share(0, 0, me).start()
    near_out(0).start()
    for k in range(1, pieces):
        for d in range(2):
            first(d, k).start()
        near_out(k).start()
    to_scalar(0, me, 0).start()

    in_tile = lax.broadcasted_iota(jnp.int32, (tile_rows, feature), 0)
    l_load.wait()
    p_load.wait()

    def fill(i, _):
        for j in range(4):
            p = i * 4 + j
            tile = pas[p].astype(jnp.float32)
            tile = jnp.where(in_tile < len_s[p], tile, tile[0:1, :])
            pas[p] = tile.astype(pas.dtype)
        return 0

    lax.fori_loop(0, per_owner // 4, fill, 0)

    def gather_max(slot, d, b, units_of):
        chosen = [wanted[d, b, my_lane + s] for s in range(cap)]
        for u in units_of:
            qs = qall[b, pl.ds(u * col, col), :]
            near = []
            for s in range(cap):
                sim = lax.dot_general(pas[chosen[s]], qs, (((1,), (1,)), ((), ())),
                                      preferred_element_type=jnp.float32)
                near.append(jnp.max(sim, axis=0, keepdims=True))
            if cap < slots:
                near.append(jnp.zeros((slots - cap, col), jnp.float32))
            near = jnp.concatenate(near, axis=0)
            high = near.astype(jnp.bfloat16).astype(jnp.float32)
            both = jnp.concatenate([high, near - high], axis=0).astype(stage.dtype)
            stage[slot, pl.ds(u * 2 * slots, 2 * slots), :] = both

    def add_up(slot, b):
        part = jnp.dot(stage[slot], fold[...], preferred_element_type=jnp.float32)
        total = None
        for u in range(units):
            at_u = u * 2 * slots
            one = part[at_u:at_u + slots] + part[at_u + slots:at_u + 2 * slots]
            if u > 0:
                one = pltpu.roll(one, u * (col // tok), 1)
            total = one if total is None else total + one
        send_buf[b] = total / float(tok)

    def take_tables(s, forward):
        for d in range(2):
            b = origin(d, s, core)
            table_hop(d, s, b).wait_recv()
            if forward is True:
                table_hop(d, s + 1, b).start()
            elif forward is not False:
                @pl.when(forward)
                def _(d=d, b=b):
                    table_hop(d, s + 1, b).start()
            table_share(d, s, b).start()
            to_scalar(d, b, 0).start()

    def own_tables(s):
        for d in range(2):
            to_scalar(d, origin(d, s, core), 0).wait()

    def sib_tables(s):
        for d in range(2):
            b = origin(d, s, 1 - core)
            table_share(d, s, b).wait_recv()
            to_scalar(d, b, 1).start()

    def sib_tables_wait(s):
        for d in range(2):
            to_scalar(d, origin(d, s, 1 - core), 1).wait()

    q_load.wait()
    to_scalar(0, me, 0).wait()
    gather_max(2, 0, me, range(units))
    table_share(0, 0, sib).wait_recv()
    to_scalar(0, sib, 1).start()
    for k in range(pieces):
        near_in(k).wait_recv()
    to_scalar(0, sib, 1).wait()
    gather_max(3, 0, sib, range(units))
    take_tables(1, True)

    def pair(s, k, c, folds=()):
        base = 0 if c is core else 2
        for slot, b in folds:
            add_up(slot, b)
        for d in range(2):
            gather_max(base + d, d, origin(d, s, c), range(*spans[k]))

    def sib_pair(s, k, folds=()):
        if k == 0:
            sib_tables_wait(s)
        for d in range(2):
            share(d, s, k, origin(d, s, 1 - core)).wait_recv()
        pair(s, k, 1 - core, folds)

    def step(s, _):
        opening = s == 1
        old = [jnp.where(opening, me, origin(0, s - 1, 1 - core)),
               jnp.where(opening, sib, origin(1, s - 1, 1 - core))]
        new = [origin(d, s, core) for d in range(2)]
        for k in range(pieces):
            for d in range(2):
                b = new[d]
                hop(d, s, k, b).wait_recv()

                @pl.when(s + 1 < half)
                def _(d=d, k=k, b=b):
                    hop(d, s + 1, k, b).start()
                share(d, s, k, b).start()

            @pl.when(s + 1 == half)
            def _(k=k):
                e = 0 if spans[k][1] <= cut else 1
                d = lax.rem(e + core, 2)
                b = at(pos + (2 * d - 1) * (half - 1), core)
                for u in range(*spans[k]):
                    end_hop(e, u, b).start()
            if k == 0:
                own_tables(s)
                sib_tables(s)
            if k == pieces - 1:
                take_tables(s + 1, s + 2 <= half)
            pair(s, k, core, [(2, old[0]), (3, old[1])] if k == 0 else ())
            if k == 0:
                score_copy(old[1]).start()

                @pl.when(s > 1)
                def _():
                    score_copy(old[0]).start()
            else:
                sib_pair(s, k - 1)
        sib_pair(s, pieces - 1, [(0, new[0]), (1, new[1])])
        for b in new:
            score_copy(b).start()
        return 0

    lax.fori_loop(1, half, step, 0)

    mine, other = at(pos + half, core), at(pos + half, 1 - core)
    own_tables(half)
    sib_tables(half)
    groups = [[t] + ([cut + t] if cut + t < units else []) for t in range(cut)]
    for t, us in enumerate(groups):
        for u in us:
            end_hop(0 if u < cut else 1, u, mine).wait_recv()
            end_share(u, mine).start()
        if t == 0:
            old = [origin(d, half - 1, 1 - core) for d in range(2)]
            for d in range(2):
                add_up(2 + d, old[d])
            gather_max(0, 0, mine, us)
            for b in old:
                score_copy(b).start()
            sib_tables_wait(half)
        else:
            gather_max(0, 0, mine, us)
            for u in groups[t - 1]:
                end_share(u, other).wait_recv()
            if t == cut - 1:
                add_up(0, mine)
            gather_max(2, 0, other, groups[t - 1])
            if t == cut - 1:
                score_copy(mine).start()
    for u in groups[-1]:
        end_share(u, other).wait_recv()
    gather_max(2, 0, other, groups[-1])
    add_up(2, other)
    score_copy(other).start()

    table_share(0, 0, me).wait_send()
    for k in range(pieces):
        near_out(k).wait_send()
        for d in range(2):
            first(d, k).wait_send()
    for d in range(2):
        table_hop(d, 1, me).wait_send()

    def drain(s, _):
        for d in range(2):
            b = origin(d, s, core)
            table_share(d, s, b).wait_send()

            @pl.when(s < half)
            def _(d=d, b=b):
                table_hop(d, s + 1, b).wait_send()
                for k in range(pieces):
                    share(d, s, k, b).wait_send()

            @pl.when(s + 1 < half)
            def _(d=d, b=b):
                for k in range(pieces):
                    hop(d, s + 1, k, b).wait_send()
        return 0

    lax.fori_loop(1, half + 1, drain, 0)
    for u in range(units):
        end_hop(0 if u < cut else 1, u, mine).wait_send()
        end_share(u, mine).wait_send()

    def each(fn):
        def body(o, _):
            fn(lax.rem(me + o, n))
            return 0
        lax.fori_loop(1, n, body, 0)

    each(lambda b: score_copy(b).wait_send())
    each(lambda b: score_in(b).wait_recv())
    got[me] = send_buf[me]
    out_ref[...] = got[...].reshape(out_ref.shape)
    place_ref[...] = place[...]


def finish(got_ref, place_ref, out_ref, best_ref):
    spread = None
    for part in split3(got_ref[...]):
        term = jnp.dot(place_ref[...], part, preferred_element_type=jnp.float32)
        spread = term if spread is None else spread + term
    queries = out_ref.shape[0]
    out_ref[...] = spread.T[:queries]
    best_ref[...] = sort_down(spread).T[:queries, :best_ref.shape[1]]


def local(ways, queries, passages, lengths, candidates):
    n = lax.axis_size("corpus")
    per_owner, tile_rows, feature = passages.shape
    per_device, tok = queries.shape[0], queries.shape[1]
    number = candidates.shape[1]
    rows = per_device * tok
    cap = max(2, 3 * number // (2 * n))
    slots = -(-cap // 8) * 8
    col = pick_tile(rows, tok)
    half = n // 4
    units = rows // col
    cfg = (n, ways, cap, per_owner, tile_rows, rows, feature, tok, col)
    dma = pltpu.SemaphoreType.DMA
    got, place = pl.pallas_call(
        functools.partial(kernel, cfg),
        out_shape=(
            jax.ShapeDtypeStruct((n * slots, 128), jnp.float32),
            jax.ShapeDtypeStruct((number, n * slots), jnp.bfloat16),
        ),
        in_specs=[pl.BlockSpec(memory_space=pl.ANY)] * 4,
        out_specs=(
            pl.BlockSpec(memory_space=pltpu.VMEM),
            pl.BlockSpec(memory_space=pltpu.VMEM),
        ),
        scratch_shapes=[
            pltpu.VMEM((n, rows, feature), queries.dtype),
            pltpu.VMEM(passages.shape, passages.dtype),
            pltpu.VMEM((1, number), jnp.int32),
            pltpu.SMEM((per_owner,), jnp.int32),
            pltpu.VMEM((2, n, n * slots // 128, 128), jnp.int32),
            pltpu.SMEM((2, n, 128), jnp.int32),
            pltpu.VMEM((number, n * slots), jnp.bfloat16),
            pltpu.VMEM((col, 128), jnp.bfloat16),
            pltpu.VMEM((4, 2 * slots * units, col), jnp.bfloat16),
            pltpu.VMEM((n, slots, 128), jnp.float32),
            pltpu.VMEM((n, slots, 128), jnp.float32),
            dma((2, half + 1, 4)), dma((2, half + 1, 4)),
            dma((2, half + 1, 4)), dma((2, half + 1, 4)),
            dma((units,)), dma((units,)),
            dma((4,)), dma((4,)),
            dma((units,)), dma((units,)),
            dma((2, half + 1)), dma((2, half + 1)),
            dma((2, half + 1)), dma((2, half + 1)),
            dma((2, 2)),
            dma((n,)), dma((n,)),
            dma((4,)),
        ],
        compiler_params=pltpu.CompilerParams(
            collective_id=0, has_side_effects=True, vmem_limit_bytes=60 * 2**20),
    )(candidates, lengths, queries.reshape(rows, feature), passages)
    return pl.pallas_call(
        finish,
        out_shape=(
            jax.ShapeDtypeStruct((per_device, number), jnp.float32),
            jax.ShapeDtypeStruct((per_device, TOPK), jnp.float32),
        ),
        in_specs=[pl.BlockSpec(memory_space=pltpu.VMEM)] * 2,
        out_specs=(pl.BlockSpec(memory_space=pltpu.VMEM), pl.BlockSpec(memory_space=pltpu.VMEM)),
    )(got, place)


def solution(mesh):
    ways = 2 if mesh.shape["groups"] == 2 else 1
    return jax.shard_map(
        functools.partial(local, ways),
        mesh=mesh,
        in_specs=(
            P(("groups", "corpus"), None, None),
            P(("groups", "corpus"), None, None),
            P(("groups", "corpus")),
            P(("groups", "corpus"), None),
        ),
        out_specs=(P(("groups", "corpus"), None), P(("groups", "corpus"), None)),
        check_vma=False,
    )
```

```python
import functools

import jax
import jax.numpy as jnp
from jax import lax
from jax.experimental import pallas as pl
from jax.experimental.pallas import tpu as pltpu
from jax.sharding import PartitionSpec as P

TOPK = 100
MESH = pl.DeviceIdType.MESH


def pick_tile(rows, tok):
    tile = 256
    while rows % tile or tile % tok:
        tile //= 2
    return tile


def sort_down(x):
    count, width = x.shape
    index = lax.broadcasted_iota(jnp.int32, (count // 8, 8, width), 0) * 8
    index = index + lax.broadcasted_iota(jnp.int32, (count // 8, 8, width), 1)
    x = x.reshape(count // 8, 8, width)
    size = 2
    while size <= count:
        gap = size // 2
        falling = (index // size) % 2 == 0
        while gap >= 1:
            low = (index // gap) % 2 == 0
            if gap >= 8:
                hop = gap // 8
                y = x.reshape(count // (2 * gap), 2, hop, 8, width)
                y = jnp.concatenate([y[:, 1:], y[:, :1]], axis=1)
                other = y.reshape(x.shape)
            else:
                other = jnp.where(low, pltpu.roll(x, 8 - gap, 1), pltpu.roll(x, gap, 1))
            x = jnp.where(low == falling, jnp.maximum(x, other), jnp.minimum(x, other))
            gap //= 2
        size *= 2
    return x.reshape(count, width)


def split3(x):
    high = x.astype(jnp.bfloat16)
    rest = x - high.astype(jnp.float32)
    mid = rest.astype(jnp.bfloat16)
    low = (rest - mid.astype(jnp.float32)).astype(jnp.bfloat16)
    return high, mid, low


def kernel(cfg, cand_hbm, len_hbm, q_hbm, p_hbm, out_ref, best_ref, qall, pas, cand_v, len_s,
           table, wanted, place, fold, stage, send_buf, got, q_sent, t_sent, sc_sent, q_recv,
           sib_recv, end_recv, tail_recv, t_recv, tsib_recv, sc_recv, sm_sem, loc_sem):
    n, ways, cap, per_owner, tile_rows, rows, feature, tok, col = cfg
    chips = n // 2
    half = chips // 2
    depth = chips // ways
    units = rows // col
    cut = (units + 1) // 2
    spans = []
    for lo, hi in ((0, cut), (cut, units)):
        mid = (lo + hi + 1) // 2
        spans += [(a, b) for a, b in ((lo, mid), (mid, hi)) if b > a]
    pieces = len(spans)
    slots = send_buf.shape[1]
    number = cand_hbm.shape[1]
    me = lax.axis_index("corpus")
    core = lax.rem(me, 2)
    chip = me // 2
    if ways == 2:
        zz, yy = chip // 2, lax.rem(chip, 2)
        pos = (1 - yy) * zz + yy * (2 * depth - 1 - zz)
    else:
        pos = chip

    def at(p, c):
        p = lax.rem(p + 2 * chips, chips)
        if ways == 2:
            far = p // depth
            p = (1 - far) * (2 * p) + far * ((2 * depth - 1 - p) * 2 + 1)
        return p * 2 + c

    sib = at(pos, 1 - core)
    toward = (at(pos + 1, core), at(pos - 1, core))

    def origin(d, s, c):
        return at(pos - s if d == 0 else pos + s, c)

    def remote(src, dst, send, recv, peer):
        return pltpu.make_async_remote_copy(
            src_ref=src, dst_ref=dst, send_sem=send, recv_sem=recv,
            device_id={"corpus": peer}, device_id_type=MESH)

    def span_of(lo, hi):
        return pl.ds(lo * col, (hi - lo) * col)

    def first(d, k):
        cut_k = span_of(*spans[k])
        return remote(q_hbm.at[cut_k, :], qall.at[me, cut_k, :],
                      q_sent.at[0], q_recv.at[d, 0, k], toward[d])

    def hop(d, s, k, b):
        piece = qall.at[b, span_of(*spans[k]), :]
        return remote(piece, piece, q_sent.at[0], q_recv.at[d, s - 1, k], toward[d])

    def share(d, s, k, b):
        piece = qall.at[b, span_of(*spans[k]), :]
        return remote(piece, piece, q_sent.at[0], sib_recv.at[d, s - 1, k], sib)

    def near_out():
        return remote(q_hbm, qall.at[me], q_sent.at[0], loc_sem.at[4], sib)

    def near_in():
        return remote(qall.at[sib], qall.at[sib], q_sent.at[0], loc_sem.at[4], sib)

    def end_hop(k, b):
        d = lax.rem((0 if spans[k][1] <= cut else 1) + core, 2)
        piece = qall.at[b, span_of(*spans[k]), :]
        return remote(piece, piece, q_sent.at[0], end_recv.at[k], at(pos + 1 - 2 * d, core))

    def end_share(k, b):
        piece = qall.at[b, span_of(*spans[k]), :]
        return remote(piece, piece, q_sent.at[0], tail_recv.at[k], sib)

    def table_hop(d, s, b):
        return remote(table.at[d, b], table.at[d, b], t_sent.at[0], t_recv.at[s - 1], toward[d])

    def table_share(d, s, b):
        return remote(table.at[d, b], table.at[d, b], t_sent.at[0], tsib_recv.at[s - 1], sib)

    def two_tables(recv):
        return remote(table.at[:, 0], table.at[:, 0], t_sent.at[0], recv, sib)

    def near_table(b):
        return remote(table.at[0, b], table.at[0, b], loc_sem.at[6], loc_sem.at[5], sib)

    my_row = me * slots // 128
    my_lane = lax.rem(me * slots, 128)

    def to_scalar(d, b, who):
        return pltpu.make_async_copy(table.at[d, b, pl.ds(my_row, 1), :],
                                     wanted.at[d, pl.ds(b, 1), :], sm_sem.at[who, d])

    def score_copy(b):
        return remote(send_buf.at[b], got.at[me], sc_sent.at[0], sc_recv.at[0], b)

    def all_scores():
        return remote(send_buf.at[pl.ds(0, n - 1)], got.at[pl.ds(0, n - 1)],
                      sc_sent.at[0], sc_recv.at[0], sib)

    barrier = pltpu.get_barrier_semaphore()
    for peer in (*toward, sib):
        pl.semaphore_signal(barrier, inc=1, device_id={"corpus": peer}, device_id_type=MESH)
    c_load = pltpu.make_async_copy(cand_hbm, cand_v, loc_sem.at[0])
    q_load = pltpu.make_async_copy(q_hbm, qall.at[me], loc_sem.at[1])
    p_load = pltpu.make_async_copy(p_hbm, pas, loc_sem.at[2])
    l_load = pltpu.make_async_copy(len_hbm, len_s, loc_sem.at[3])
    c_load.start()
    l_load.start()
    p_load.start()
    q_load.start()
    pl.semaphore_wait(barrier, 3)
    for d in range(2):
        first(d, 0).start()

    c_load.wait()
    across = jnp.broadcast_to(cand_v[...], (number, number))
    down = across.T
    down_owner = lax.div(down, per_owner)
    local_id = down[:, :1] - down_owner[:, :1] * per_owner
    r_at = lax.broadcasted_iota(jnp.int32, (number, number), 0)
    c_at = lax.broadcasted_iota(jnp.int32, (number, number), 1)
    ahead = jnp.where((lax.div(across, per_owner) == down_owner) & (c_at < r_at), 1.0, 0.0)
    slot = down_owner[:, :1].astype(jnp.float32) * float(slots) + jnp.sum(ahead, axis=1, keepdims=True)
    slot_at = lax.broadcasted_iota(jnp.int32, place.shape, 1).astype(jnp.float32)
    spot = slot_at == slot
    line = jnp.max(jnp.where(spot, local_id, 0), axis=0, keepdims=True)
    line = jnp.concatenate([line[:, i * 128:(i + 1) * 128] for i in range(n * slots // 128)], axis=0)
    for d in range(2):
        table[d, me] = line
    place[...] = jnp.where(spot, 1.0, 0.0).astype(place.dtype)
    row_at = lax.broadcasted_iota(jnp.int32, (col, 128), 0) // tok
    lane_at = lax.broadcasted_iota(jnp.int32, (col, 128), 1)
    fold[...] = jnp.where(row_at == lane_at, 1.0, 0.0).astype(fold.dtype)
    for d in range(2):
        table_hop(d, 1, me).start()
    near_table(me).start()
    near_out().start()
    for k in range(1, pieces):
        for d in range(2):
            first(d, k).start()
    to_scalar(0, me, 0).start()

    in_tile = lax.broadcasted_iota(jnp.int32, (tile_rows, feature), 0)
    l_load.wait()
    p_load.wait()

    def fill(i, _):
        for j in range(4):
            p = i * 4 + j
            tile = pas[p].astype(jnp.float32)
            tile = jnp.where(in_tile < len_s[p], tile, tile[0:1, :])
            pas[p] = tile.astype(pas.dtype)
        return 0

    lax.fori_loop(0, per_owner // 4, fill, 0)

    def gather_max(slot, d, b, units_of):
        chosen = [wanted[d, b, my_lane + s] for s in range(cap)]
        for u in units_of:
            qs = qall[b, pl.ds(u * col, col), :]
            near = []
            for s in range(cap):
                sim = lax.dot_general(pas[chosen[s]], qs, (((1,), (1,)), ((), ())),
                                      preferred_element_type=jnp.float32)
                near.append(jnp.max(sim, axis=0, keepdims=True))
            if cap < slots:
                near.append(jnp.zeros((slots - cap, col), jnp.float32))
            near = jnp.concatenate(near, axis=0)
            high = near.astype(jnp.bfloat16).astype(jnp.float32)
            both = jnp.concatenate([high, near - high], axis=0).astype(stage.dtype)
            stage[slot, pl.ds(u * 2 * slots, 2 * slots), :] = both

    def add_up(slot, b):
        part = jnp.dot(stage[slot], fold[...], preferred_element_type=jnp.float32)
        total = None
        for u in range(units):
            at_u = u * 2 * slots
            one = part[at_u:at_u + slots] + part[at_u + slots:at_u + 2 * slots]
            if u > 0:
                one = pltpu.roll(one, u * (col // tok), 1)
            total = one if total is None else total + one
        send_buf[b] = total / float(tok)

    def take_tables(s):
        two_tables(t_recv.at[s - 1]).wait_recv()
        for d in range(2):
            b = origin(d, s, core)

            @pl.when(s < half)
            def _(d=d, b=b):
                table_hop(d, s + 1, b).start()
            table_share(d, s, b).start()
            to_scalar(d, b, 0).start()

    def own_tables(s):
        for d in range(2):
            to_scalar(d, origin(d, s, core), 0).wait()

    def sib_tables(s):
        two_tables(tsib_recv.at[s - 1]).wait_recv()
        for d in range(2):
            to_scalar(d, origin(d, s, 1 - core), 1).start()

    def sib_tables_wait(s):
        for d in range(2):
            to_scalar(d, origin(d, s, 1 - core), 1).wait()

    q_load.wait()
    to_scalar(0, me, 0).wait()
    gather_max(2, 0, me, range(units))
    near_table(sib).wait_recv()
    to_scalar(0, sib, 1).start()
    near_in().wait_recv()
    to_scalar(0, sib, 1).wait()
    gather_max(3, 0, sib, range(units))
    take_tables(1)

    def pair(s, k, c, folds=()):
        base = 0 if c is core else 2
        for slot, b in folds:
            add_up(slot, b)
        for d in range(2):
            gather_max(base + d, d, origin(d, s, c), range(*spans[k]))

    def sib_pair(s, k, folds=()):
        if k == 0:
            sib_tables_wait(s)
        for d in range(2):
            share(d, s, k, origin(d, s, 1 - core)).wait_recv()
        pair(s, k, 1 - core, folds)

    def step(s, _):
        opening = s == 1
        old = [jnp.where(opening, me, origin(0, s - 1, 1 - core)),
               jnp.where(opening, sib, origin(1, s - 1, 1 - core))]
        new = [origin(d, s, core) for d in range(2)]
        for k in range(pieces):
            for d in range(2):
                b = new[d]
                hop(d, s, k, b).wait_recv()

                @pl.when(s + 1 < half)
                def _(d=d, k=k, b=b):
                    hop(d, s + 1, k, b).start()
                share(d, s, k, b).start()

            @pl.when(s + 1 == half)
            def _(k=k):
                d = lax.rem((0 if spans[k][1] <= cut else 1) + core, 2)
                end_hop(k, at(pos + (2 * d - 1) * (half - 1), core)).start()
            if k == 0:
                own_tables(s)
                sib_tables(s)
            if k == pieces - 1:
                take_tables(s + 1)
            pair(s, k, core, [(2, old[0]), (3, old[1])] if k == 0 else ())
            if k == 0:
                score_copy(old[1]).start()

                @pl.when(s > 1)
                def _():
                    score_copy(old[0]).start()
            sib_pair(s, k, [(0, new[0]), (1, new[1])] if k == pieces - 1 else ())
        for b in new:
            score_copy(b).start()
        return 0

    lax.fori_loop(1, half, step, 0)

    mine, other = at(pos + half, core), at(pos + half, 1 - core)
    own_tables(half)
    sib_tables(half)
    early = [k for k in range(pieces) if spans[k][1] <= cut]
    late = [k for k in range(pieces) if spans[k][1] > cut]
    groups = [[x[t] for x in (early, late) if t < len(x)] for t in range(max(len(early), len(late)))]

    def units_of(ks):
        return [u for k in ks for u in range(*spans[k])]

    for t, ks in enumerate(groups):
        for k in ks:
            end_hop(k, mine).wait_recv()
            end_share(k, mine).start()
        if t == 0:
            old = [origin(d, half - 1, 1 - core) for d in range(2)]
            for d in range(2):
                add_up(2 + d, old[d])
        gather_max(0, 0, mine, units_of(ks))
        if t == 0:
            for b in old:
                score_copy(b).start()
            sib_tables_wait(half)
        for k in ks:
            end_share(k, other).wait_recv()
        if t == len(groups) - 1:
            add_up(0, mine)
        gather_max(2, 0, other, units_of(ks))
    score_copy(mine).start()
    add_up(2, other)
    score_copy(other).start()

    remote(qall.at[pl.ds(0, n - 1)], qall.at[pl.ds(0, n - 1)], q_sent.at[0], loc_sem.at[4],
           sib).wait_send()
    remote(table.at[:, pl.ds(0, n // 2)], table.at[:, pl.ds(0, n // 2)], t_sent.at[0],
           loc_sem.at[5], sib).wait_send()
    near_table(me).wait_send()
    all_scores().wait_send()
    all_scores().wait_recv()
    got[me] = send_buf[me]
    spread = None
    for part in split3(got[...].reshape(n * slots, 128)):
        term = jnp.dot(place[...], part, preferred_element_type=jnp.float32)
        spread = term if spread is None else spread + term
    queries = out_ref.shape[0]
    out_ref[...] = spread.T[:queries]
    best_ref[...] = sort_down(spread).T[:queries, :best_ref.shape[1]]


def local(ways, queries, passages, lengths, candidates):
    n = lax.axis_size("corpus")
    per_owner, tile_rows, feature = passages.shape
    per_device, tok = queries.shape[0], queries.shape[1]
    number = candidates.shape[1]
    rows = per_device * tok
    cap = max(2, 3 * number // (2 * n))
    slots = -(-cap // 8) * 8
    col = pick_tile(rows, tok)
    half = n // 4
    units = rows // col
    cfg = (n, ways, cap, per_owner, tile_rows, rows, feature, tok, col)
    dma = pltpu.SemaphoreType.DMA
    return pl.pallas_call(
        functools.partial(kernel, cfg),
        out_shape=(
            pltpu.VMEM((per_device, number), jnp.float32),
            pltpu.VMEM((per_device, TOPK), jnp.float32),
        ),
        in_specs=[pl.BlockSpec(memory_space=pl.ANY)] * 4,
        out_specs=(
            pl.BlockSpec(memory_space=pltpu.VMEM),
            pl.BlockSpec(memory_space=pltpu.VMEM),
        ),
        scratch_shapes=[
            pltpu.VMEM((n, rows, feature), queries.dtype),
            pltpu.VMEM(passages.shape, passages.dtype),
            pltpu.VMEM((1, number), jnp.int32),
            pltpu.SMEM((per_owner,), jnp.int32),
            pltpu.VMEM((2, n, n * slots // 128, 128), jnp.int32),
            pltpu.SMEM((2, n, 128), jnp.int32),
            pltpu.VMEM((number, n * slots), jnp.bfloat16),
            pltpu.VMEM((col, 128), jnp.bfloat16),
            pltpu.VMEM((4, 2 * slots * units, col), jnp.bfloat16),
            pltpu.VMEM((n, slots, 128), jnp.float32),
            pltpu.VMEM((n, slots, 128), jnp.float32),
            dma((1,)), dma((1,)), dma((1,)),
            dma((2, half - 1, 4)), dma((2, half - 1, 4)),
            dma((4,)), dma((4,)),
            dma((half,)), dma((half,)),
            dma((1,)),
            dma((2, 2)),
            dma((7,)),
        ],
        compiler_params=pltpu.CompilerParams(
            collective_id=0, has_side_effects=True, vmem_limit_bytes=60 * 2**20),
    )(candidates, lengths, queries.reshape(rows, feature), passages)


def solution(mesh):
    ways = 2 if mesh.shape["groups"] == 2 else 1
    return jax.shard_map(
        functools.partial(local, ways),
        mesh=mesh,
        in_specs=(
            P(("groups", "corpus"), None, None),
            P(("groups", "corpus"), None, None),
            P(("groups", "corpus")),
            P(("groups", "corpus"), None),
        ),
        out_specs=(P(("groups", "corpus"), None), P(("groups", "corpus"), None)),
        check_vma=False,
    )
```

```python
import functools

import jax
import jax.numpy as jnp
from jax import lax
from jax.experimental import pallas as pl
from jax.experimental.pallas import tpu as pltpu
from jax.sharding import PartitionSpec as P

TOPK = 100
MESH = pl.DeviceIdType.MESH


def pick_tile(rows, tok):
    tile = 256
    while rows % tile or tile % tok:
        tile //= 2
    return tile


def sort_down(x):
    count, width = x.shape
    index = lax.broadcasted_iota(jnp.int32, (count // 8, 8, width), 0) * 8
    index = index + lax.broadcasted_iota(jnp.int32, (count // 8, 8, width), 1)
    x = x.reshape(count // 8, 8, width)
    size = 2
    while size <= count:
        gap = size // 2
        falling = (index // size) % 2 == 0
        while gap >= 1:
            low = (index // gap) % 2 == 0
            if gap >= 8:
                hop = gap // 8
                y = x.reshape(count // (2 * gap), 2, hop, 8, width)
                y = jnp.concatenate([y[:, 1:], y[:, :1]], axis=1)
                other = y.reshape(x.shape)
            else:
                other = jnp.where(low, pltpu.roll(x, 8 - gap, 1), pltpu.roll(x, gap, 1))
            x = jnp.where(low == falling, jnp.maximum(x, other), jnp.minimum(x, other))
            gap //= 2
        size *= 2
    return x.reshape(count, width)


def split3(x):
    high = x.astype(jnp.bfloat16)
    rest = x - high.astype(jnp.float32)
    mid = rest.astype(jnp.bfloat16)
    low = (rest - mid.astype(jnp.float32)).astype(jnp.bfloat16)
    return high, mid, low


def kernel(cfg, cand_hbm, len_hbm, q_hbm, p_hbm, out_ref, best_ref, qall, pas, cand_v, len_s,
           table, wanted, place, fold, stage, send_buf, got, q_sent, t_sent, sc_sent, q_recv,
           sib_recv, end_recv, tail_recv, t_recv, tsib_recv, sc_recv, sm_sem, loc_sem):
    n, ways, cap, per_owner, tile_rows, rows, feature, tok, col = cfg
    chips = n // 2
    half = chips // 2
    depth = chips // ways
    units = rows // col
    cut = (units + 1) // 2
    spans = []
    for lo, hi in ((0, cut), (cut, units)):
        mid = (lo + hi + 1) // 2
        spans += [(a, b) for a, b in ((lo, mid), (mid, hi)) if b > a]
    pieces = len(spans)
    early = [k for k in range(pieces) if spans[k][1] <= cut]
    late = [k for k in range(pieces) if spans[k][1] > cut]
    order = (early + late, late + early)
    slots = send_buf.shape[1]
    number = cand_hbm.shape[1]
    me = lax.axis_index("corpus")
    core = lax.rem(me, 2)
    chip = me // 2
    if ways == 2:
        zz, yy = chip // 2, lax.rem(chip, 2)
        pos = (1 - yy) * zz + yy * (2 * depth - 1 - zz)
    else:
        pos = chip

    def at(p, c):
        p = lax.rem(p + 2 * chips, chips)
        if ways == 2:
            far = p // depth
            p = (1 - far) * (2 * p) + far * ((2 * depth - 1 - p) * 2 + 1)
        return p * 2 + c

    sib = at(pos, 1 - core)

    def sign(e, c):
        return 1 - 2 * lax.rem(e + c, 2)

    toward = (at(pos + sign(0, core), core), at(pos + sign(1, core), core))

    def origin(e, s, c):
        return at(pos - sign(e, c) * s, c)

    def remote(src, dst, send, recv, peer):
        return pltpu.make_async_remote_copy(
            src_ref=src, dst_ref=dst, send_sem=send, recv_sem=recv,
            device_id={"corpus": peer}, device_id_type=MESH)

    def span_of(lo, hi):
        return pl.ds(lo * col, (hi - lo) * col)

    def first(d, k):
        cut_k = span_of(*spans[order[d][k]])
        return remote(q_hbm.at[cut_k, :], qall.at[me, cut_k, :],
                      q_sent.at[0], q_recv.at[d, 0, k], toward[d])

    def hop(d, s, k, b):
        piece = qall.at[b, span_of(*spans[order[d][k]]), :]
        return remote(piece, piece, q_sent.at[0], q_recv.at[d, s - 1, k], toward[d])

    def share(d, s, k, b):
        piece = qall.at[b, span_of(*spans[order[d][k]]), :]
        return remote(piece, piece, q_sent.at[0], sib_recv.at[d, s - 1, k], sib)

    def near_out():
        return remote(q_hbm, qall.at[me], q_sent.at[0], loc_sem.at[4], sib)

    def near_in():
        return remote(qall.at[sib], qall.at[sib], q_sent.at[0], loc_sem.at[4], sib)

    def end_hop(u, b):
        piece = qall.at[b, span_of(u, u + 1), :]
        return remote(piece, piece, q_sent.at[0], end_recv.at[u], toward[0 if u < cut else 1])

    def end_share(u, b):
        piece = qall.at[b, span_of(u, u + 1), :]
        return remote(piece, piece, q_sent.at[0], tail_recv.at[u], sib)

    def table_hop(d, s, b):
        return remote(table.at[d, b], table.at[d, b], t_sent.at[0], t_recv.at[s - 1], toward[d])

    def table_share(d, s, b):
        return remote(table.at[d, b], table.at[d, b], t_sent.at[0], tsib_recv.at[s - 1], sib)

    def two_tables(recv):
        return remote(table.at[:, 0], table.at[:, 0], t_sent.at[0], recv, sib)

    def near_table(b):
        return remote(table.at[0, b], table.at[0, b], loc_sem.at[6], loc_sem.at[5], sib)

    my_row = me * slots // 128
    my_lane = lax.rem(me * slots, 128)

    def to_scalar(d, b, who):
        return pltpu.make_async_copy(table.at[d, b, pl.ds(my_row, 1), :],
                                     wanted.at[d, pl.ds(b, 1), :], sm_sem.at[who, d])

    def score_copy(b):
        return remote(send_buf.at[b], got.at[me], sc_sent.at[0], sc_recv.at[0], b)

    def all_scores():
        return remote(send_buf.at[pl.ds(0, n - 1)], got.at[pl.ds(0, n - 1)],
                      sc_sent.at[0], sc_recv.at[0], sib)

    barrier = pltpu.get_barrier_semaphore()
    for peer in (*toward, sib):
        pl.semaphore_signal(barrier, inc=1, device_id={"corpus": peer}, device_id_type=MESH)
    c_load = pltpu.make_async_copy(cand_hbm, cand_v, loc_sem.at[0])
    q_load = pltpu.make_async_copy(q_hbm, qall.at[me], loc_sem.at[1])
    p_load = pltpu.make_async_copy(p_hbm, pas, loc_sem.at[2])
    l_load = pltpu.make_async_copy(len_hbm, len_s, loc_sem.at[3])
    c_load.start()
    l_load.start()
    pl.semaphore_wait(barrier, 3)
    for d in range(2):
        first(d, 0).start()
    p_load.start()
    q_load.start()

    c_load.wait()
    across = jnp.broadcast_to(cand_v[...], (number, number))
    down = across.T
    down_owner = lax.div(down, per_owner)
    local_id = down[:, :1] - down_owner[:, :1] * per_owner
    r_at = lax.broadcasted_iota(jnp.int32, (number, number), 0)
    c_at = lax.broadcasted_iota(jnp.int32, (number, number), 1)
    ahead = jnp.where((lax.div(across, per_owner) == down_owner) & (c_at < r_at), 1.0, 0.0)
    slot = down_owner[:, :1].astype(jnp.float32) * float(slots) + jnp.sum(ahead, axis=1, keepdims=True)
    slot_at = lax.broadcasted_iota(jnp.int32, place.shape, 1).astype(jnp.float32)
    spot = slot_at == slot
    line = jnp.max(jnp.where(spot, local_id, 0), axis=0, keepdims=True)
    line = jnp.concatenate([line[:, i * 128:(i + 1) * 128] for i in range(n * slots // 128)], axis=0)
    for d in range(2):
        table[d, me] = line
    place[...] = jnp.where(spot, 1.0, 0.0).astype(place.dtype)
    row_at = lax.broadcasted_iota(jnp.int32, (col, 128), 0) // tok
    lane_at = lax.broadcasted_iota(jnp.int32, (col, 128), 1)
    fold[...] = jnp.where(row_at == lane_at, 1.0, 0.0).astype(fold.dtype)
    for d in range(2):
        table_hop(d, 1, me).start()
    near_table(me).start()
    near_out().start()
    for k in range(1, pieces):
        for d in range(2):
            first(d, k).start()
    to_scalar(0, me, 0).start()

    in_tile = lax.broadcasted_iota(jnp.int32, (tile_rows, feature), 0)
    l_load.wait()
    p_load.wait()

    def fill(i, _):
        for j in range(4):
            p = i * 4 + j
            tile = pas[p].astype(jnp.float32)
            tile = jnp.where(in_tile < len_s[p], tile, tile[0:1, :])
            pas[p] = tile.astype(pas.dtype)
        return 0

    lax.fori_loop(0, per_owner // 4, fill, 0)

    def gather_max(slot, d, b, units_of):
        chosen = [wanted[d, b, my_lane + s] for s in range(cap)]
        for u in units_of:
            qs = qall[b, pl.ds(u * col, col), :]
            near = []
            for s in range(cap):
                sim = lax.dot_general(pas[chosen[s]], qs, (((1,), (1,)), ((), ())),
                                      preferred_element_type=jnp.float32)
                near.append(jnp.max(sim, axis=0, keepdims=True))
            if cap < slots:
                near.append(jnp.zeros((slots - cap, col), jnp.float32))
            near = jnp.concatenate(near, axis=0)
            high = near.astype(jnp.bfloat16).astype(jnp.float32)
            both = jnp.concatenate([high, near - high], axis=0).astype(stage.dtype)
            stage[slot, pl.ds(u * 2 * slots, 2 * slots), :] = both

    def add_up(slot, b):
        part = jnp.dot(stage[slot], fold[...], preferred_element_type=jnp.float32)
        total = None
        for u in range(units):
            at_u = u * 2 * slots
            one = part[at_u:at_u + slots] + part[at_u + slots:at_u + 2 * slots]
            if u > 0:
                one = pltpu.roll(one, u * (col // tok), 1)
            total = one if total is None else total + one
        send_buf[b] = total / float(tok)

    def take_tables(s):
        two_tables(t_recv.at[s - 1]).wait_recv()
        for d in range(2):
            b = origin(d, s, core)

            @pl.when(s < half)
            def _(d=d, b=b):
                table_hop(d, s + 1, b).start()
            table_share(d, s, b).start()
            to_scalar(d, b, 0).start()

    def own_tables(s):
        for d in range(2):
            to_scalar(d, origin(d, s, core), 0).wait()

    def sib_tables(s):
        two_tables(tsib_recv.at[s - 1]).wait_recv()
        for d in range(2):
            to_scalar(d, origin(d, s, 1 - core), 1).start()

    def sib_tables_wait(s):
        for d in range(2):
            to_scalar(d, origin(d, s, 1 - core), 1).wait()

    q_load.wait()
    to_scalar(0, me, 0).wait()
    gather_max(2, 0, me, range(units))
    near_table(sib).wait_recv()
    to_scalar(0, sib, 1).start()
    near_in().wait_recv()
    to_scalar(0, sib, 1).wait()
    gather_max(3, 0, sib, range(units))
    take_tables(1)

    def pair(s, k, c, folds=()):
        base = 0 if c is core else 2
        for slot, b in folds:
            add_up(slot, b)
        for d in range(2):
            gather_max(base + d, d, origin(d, s, c), range(*spans[order[d][k]]))

    def sib_pair(s, k, folds=()):
        if k == 0:
            sib_tables_wait(s)
        for d in range(2):
            share(d, s, k, origin(d, s, 1 - core)).wait_recv()
        pair(s, k, 1 - core, folds)

    def step(s, _):
        opening = s == 1
        old = [jnp.where(opening, me, origin(0, s - 1, 1 - core)),
               jnp.where(opening, sib, origin(1, s - 1, 1 - core))]
        new = [origin(d, s, core) for d in range(2)]
        for k in range(pieces):
            for d in range(2):
                b = new[d]
                hop(d, s, k, b).wait_recv()

                @pl.when(s + 1 < half)
                def _(d=d, k=k, b=b):
                    hop(d, s + 1, k, b).start()
                share(d, s, k, b).start()

            ends = [(d, order[d][k]) for d in range(2)
                    if order[d][k] in (early, late)[d]]
            if ends:
                @pl.when(s + 1 == half)
                def _(ends=ends):
                    for j in range(2):
                        for d, p in ends:
                            if spans[p][0] + j < spans[p][1]:
                                end_hop(spans[p][0] + j, new[d]).start()
            if k == 0:
                own_tables(s)
                sib_tables(s)
            if k == pieces - 1:
                take_tables(s + 1)
            pair(s, k, core, [(2, old[0]), (3, old[1])] if k == 0 else ())
            if k == 0:
                score_copy(old[1]).start()

                @pl.when(s > 1)
                def _():
                    score_copy(old[0]).start()
            sib_pair(s, k, [(0, new[0]), (1, new[1])] if k == pieces - 1 else ())
        for b in new:
            score_copy(b).start()
        return 0

    lax.fori_loop(1, half, step, 0)

    mine, other = at(pos + half, core), at(pos + half, 1 - core)
    own_tables(half)
    sib_tables(half)
    groups = [[t] + ([cut + t] if cut + t < units else []) for t in range(cut)]
    for t, us in enumerate(groups):
        for u in us:
            end_hop(u, mine).wait_recv()
            end_share(u, mine).start()
        if t == 0:
            old = [origin(d, half - 1, 1 - core) for d in range(2)]
            for d in range(2):
                add_up(2 + d, old[d])
        gather_max(0, 0, mine, us)
        if t == 0:
            for b in old:
                score_copy(b).start()
            sib_tables_wait(half)
        else:
            for u in groups[t - 1]:
                end_share(u, other).wait_recv()
            if t == cut - 1:
                add_up(0, mine)
            gather_max(2, 0, other, groups[t - 1])
    score_copy(mine).start()
    for u in groups[-1]:
        end_share(u, other).wait_recv()
    gather_max(2, 0, other, groups[-1])
    add_up(2, other)
    score_copy(other).start()

    remote(qall.at[pl.ds(0, n - 1)], qall.at[pl.ds(0, n - 1)], q_sent.at[0], loc_sem.at[4],
           sib).wait_send()
    remote(table.at[:, pl.ds(0, n // 2)], table.at[:, pl.ds(0, n // 2)], t_sent.at[0],
           loc_sem.at[5], sib).wait_send()
    near_table(me).wait_send()
    all_scores().wait_send()
    all_scores().wait_recv()
    got[me] = send_buf[me]
    spread = None
    for part in split3(got[...].reshape(n * slots, 128)):
        term = jnp.dot(place[...], part, preferred_element_type=jnp.float32)
        spread = term if spread is None else spread + term
    queries = out_ref.shape[0]
    out_ref[...] = spread.T[:queries]
    best_ref[...] = sort_down(spread).T[:queries, :best_ref.shape[1]]


def hand_out(scores_ref, best_ref, scores_hbm, best_hbm, sem):
    moves = [pltpu.make_async_copy(scores_ref, scores_hbm, sem.at[0]),
             pltpu.make_async_copy(best_ref, best_hbm, sem.at[1])]
    for move in moves:
        move.start()
    for move in moves:
        move.wait()


def local(ways, queries, passages, lengths, candidates):
    n = lax.axis_size("corpus")
    per_owner, tile_rows, feature = passages.shape
    per_device, tok = queries.shape[0], queries.shape[1]
    number = candidates.shape[1]
    rows = per_device * tok
    cap = max(2, 3 * number // (2 * n))
    slots = -(-cap // 8) * 8
    col = pick_tile(rows, tok)
    half = n // 4
    units = rows // col
    cfg = (n, ways, cap, per_owner, tile_rows, rows, feature, tok, col)
    dma = pltpu.SemaphoreType.DMA
    scores, best = pl.pallas_call(
        functools.partial(kernel, cfg),
        out_shape=(
            pltpu.VMEM((per_device, number), jnp.float32),
            pltpu.VMEM((per_device, TOPK), jnp.float32),
        ),
        in_specs=[pl.BlockSpec(memory_space=pl.ANY)] * 4,
        out_specs=(
            pl.BlockSpec(memory_space=pltpu.VMEM),
            pl.BlockSpec(memory_space=pltpu.VMEM),
        ),
        scratch_shapes=[
            pltpu.VMEM((n, rows, feature), queries.dtype),
            pltpu.VMEM(passages.shape, passages.dtype),
            pltpu.VMEM((1, number), jnp.int32),
            pltpu.SMEM((per_owner,), jnp.int32),
            pltpu.VMEM((2, n, n * slots // 128, 128), jnp.int32),
            pltpu.SMEM((2, n, 128), jnp.int32),
            pltpu.VMEM((number, n * slots), jnp.bfloat16),
            pltpu.VMEM((col, 128), jnp.bfloat16),
            pltpu.VMEM((4, 2 * slots * units, col), jnp.bfloat16),
            pltpu.VMEM((n, slots, 128), jnp.float32),
            pltpu.VMEM((n, slots, 128), jnp.float32),
            dma((1,)), dma((1,)), dma((1,)),
            dma((2, half - 1, 4)), dma((2, half - 1, 4)),
            dma((units,)), dma((units,)),
            dma((half,)), dma((half,)),
            dma((1,)),
            dma((2, 2)),
            dma((7,)),
        ],
        compiler_params=pltpu.CompilerParams(
            collective_id=0, has_side_effects=True, vmem_limit_bytes=60 * 2**20),
    )(candidates, lengths, queries.reshape(rows, feature), passages)
    scores = pltpu.with_memory_space_constraint(scores, pltpu.VMEM)
    best = pltpu.with_memory_space_constraint(best, pltpu.VMEM)
    return pl.pallas_call(
        hand_out,
        out_shape=(
            jax.ShapeDtypeStruct((per_device, number), jnp.float32),
            jax.ShapeDtypeStruct((per_device, TOPK), jnp.float32),
        ),
        in_specs=[pl.BlockSpec(memory_space=pltpu.VMEM)] * 2,
        out_specs=(pl.BlockSpec(memory_space=pl.ANY), pl.BlockSpec(memory_space=pl.ANY)),
        scratch_shapes=[dma((2,))],
    )(scores, best)


def solution(mesh):
    ways = 2 if mesh.shape["groups"] == 2 else 1
    return jax.shard_map(
        functools.partial(local, ways),
        mesh=mesh,
        in_specs=(
            P(("groups", "corpus"), None, None),
            P(("groups", "corpus"), None, None),
            P(("groups", "corpus")),
            P(("groups", "corpus"), None),
        ),
        out_specs=(P(("groups", "corpus"), None), P(("groups", "corpus"), None)),
        check_vma=False,
    )
```

```python
import functools

import jax
import jax.numpy as jnp
from jax import lax
from jax.experimental import pallas as pl
from jax.experimental.pallas import tpu as pltpu
from jax.sharding import PartitionSpec as P

TOPK = 100
MESH = pl.DeviceIdType.MESH


def pick_tile(rows, tok):
    tile = 256
    while rows % tile or tile % tok:
        tile //= 2
    return tile


def sort_down(x):
    count, width = x.shape
    index = lax.broadcasted_iota(jnp.int32, (count // 8, 8, width), 0) * 8
    index = index + lax.broadcasted_iota(jnp.int32, (count // 8, 8, width), 1)
    x = x.reshape(count // 8, 8, width)
    size = 2
    while size <= count:
        gap = size // 2
        falling = (index // size) % 2 == 0
        while gap >= 1:
            low = (index // gap) % 2 == 0
            if gap >= 8:
                hop = gap // 8
                y = x.reshape(count // (2 * gap), 2, hop, 8, width)
                y = jnp.concatenate([y[:, 1:], y[:, :1]], axis=1)
                other = y.reshape(x.shape)
            else:
                other = jnp.where(low, pltpu.roll(x, 8 - gap, 1), pltpu.roll(x, gap, 1))
            x = jnp.where(low == falling, jnp.maximum(x, other), jnp.minimum(x, other))
            gap //= 2
        size *= 2
    return x.reshape(count, width)


def split3(x):
    high = x.astype(jnp.bfloat16)
    rest = x - high.astype(jnp.float32)
    mid = rest.astype(jnp.bfloat16)
    low = (rest - mid.astype(jnp.float32)).astype(jnp.bfloat16)
    return high, mid, low


def kernel(cfg, cand_hbm, len_hbm, q_hbm, p_hbm, out_ref, best_ref, qall, pas, cand_v, len_s,
           table, wanted, place, fold, stage, send_buf, got, q_sent, t_sent, sc_sent, q_recv,
           sib_recv, end_recv, tail_recv, t_recv, tsib_recv, sc_recv, sm_sem, loc_sem):
    n, ways, cap, per_owner, tile_rows, rows, feature, tok, col = cfg
    chips = n // 2
    half = chips // 2
    depth = chips // ways
    units = rows // col
    cut = (units + 1) // 2
    spans = []
    for lo, hi in ((0, cut), (cut, units)):
        mid = (lo + hi + 1) // 2
        spans += [(a, b) for a, b in ((lo, mid), (mid, hi)) if b > a]
    pieces = len(spans)
    early = [k for k in range(pieces) if spans[k][1] <= cut]
    late = [k for k in range(pieces) if spans[k][1] > cut]
    order = (early + late, late + early)
    slots = send_buf.shape[1]
    number = cand_hbm.shape[1]
    me = lax.axis_index("corpus")
    core = lax.rem(me, 2)
    chip = me // 2
    if ways == 2:
        zz, yy = chip // 2, lax.rem(chip, 2)
        pos = (1 - yy) * zz + yy * (2 * depth - 1 - zz)
    else:
        pos = chip

    def at(p, c):
        p = lax.rem(p + 2 * chips, chips)
        if ways == 2:
            far = p // depth
            p = (1 - far) * (2 * p) + far * ((2 * depth - 1 - p) * 2 + 1)
        return p * 2 + c

    sib = at(pos, 1 - core)

    def sign(e, c):
        return 1 - 2 * lax.rem(e + c, 2)

    toward = (at(pos + sign(0, core), core), at(pos + sign(1, core), core))

    def origin(e, s, c):
        return at(pos - sign(e, c) * s, c)

    def remote(src, dst, send, recv, peer):
        return pltpu.make_async_remote_copy(
            src_ref=src, dst_ref=dst, send_sem=send, recv_sem=recv,
            device_id={"corpus": peer}, device_id_type=MESH)

    def span_of(lo, hi):
        return pl.ds(lo * col, (hi - lo) * col)

    def first(d, k):
        cut_k = span_of(*spans[order[d][k]])
        return remote(q_hbm.at[cut_k, :], qall.at[me, cut_k, :],
                      q_sent.at[0], q_recv.at[d, 0, k], toward[d])

    def hop(d, s, k, b):
        piece = qall.at[b, span_of(*spans[order[d][k]]), :]
        return remote(piece, piece, q_sent.at[0], q_recv.at[d, s - 1, k], toward[d])

    def share(d, s, k, b):
        piece = qall.at[b, span_of(*spans[order[d][k]]), :]
        return remote(piece, piece, q_sent.at[0], sib_recv.at[s - 1, k], sib)

    def near_out():
        return remote(q_hbm, qall.at[me], q_sent.at[0], loc_sem.at[4], sib)

    def near_in():
        return remote(qall.at[sib], qall.at[sib], q_sent.at[0], loc_sem.at[4], sib)

    def end_hop(k, b):
        piece = qall.at[b, span_of(*spans[k]), :]
        return remote(piece, piece, q_sent.at[0], end_recv.at[k], toward[0 if k in early else 1])

    def end_share(t, k, b):
        piece = qall.at[b, span_of(*spans[k]), :]
        return remote(piece, piece, q_sent.at[0], tail_recv.at[t], sib)

    def so_many(count, recv):
        piece = qall.at[0, span_of(0, count), :]
        return remote(piece, piece, q_sent.at[0], recv, sib)

    def table_hop(d, s, b):
        return remote(table.at[d, b], table.at[d, b], t_sent.at[0], t_recv.at[s - 1], toward[d])

    def table_share(d, s, b):
        return remote(table.at[d, b], table.at[d, b], t_sent.at[0], tsib_recv.at[s - 1], sib)

    def two_tables(recv):
        return remote(table.at[:, 0], table.at[:, 0], t_sent.at[0], recv, sib)

    def near_table(b):
        return remote(table.at[0, b], table.at[0, b], loc_sem.at[6], loc_sem.at[5], sib)

    my_row = me * slots // 128
    my_lane = lax.rem(me * slots, 128)

    def to_scalar(d, b, who):
        return pltpu.make_async_copy(table.at[d, b, pl.ds(my_row, 1), :],
                                     wanted.at[d, pl.ds(b, 1), :], sm_sem.at[who, d])

    def score_copy(b):
        return remote(send_buf.at[b], got.at[me], sc_sent.at[0], sc_recv.at[0], b)

    def all_scores():
        return remote(send_buf.at[pl.ds(0, n - 1)], got.at[pl.ds(0, n - 1)],
                      sc_sent.at[0], sc_recv.at[0], sib)

    barrier = pltpu.get_barrier_semaphore()
    for peer in (*toward, sib):
        pl.semaphore_signal(barrier, inc=1, device_id={"corpus": peer}, device_id_type=MESH)
    c_load = pltpu.make_async_copy(cand_hbm, cand_v, loc_sem.at[0])
    q_load = pltpu.make_async_copy(q_hbm, qall.at[me], loc_sem.at[1])
    p_load = pltpu.make_async_copy(p_hbm, pas, loc_sem.at[2])
    l_load = pltpu.make_async_copy(len_hbm, len_s, loc_sem.at[3])
    c_load.start()
    l_load.start()
    pl.semaphore_wait(barrier, 3)
    for d in range(2):
        first(d, 0).start()
    p_load.start()
    q_load.start()

    c_load.wait()
    across = jnp.broadcast_to(cand_v[...], (number, number))
    down = across.T
    down_owner = lax.div(down, per_owner)
    local_id = down[:, :1] - down_owner[:, :1] * per_owner
    r_at = lax.broadcasted_iota(jnp.int32, (number, number), 0)
    c_at = lax.broadcasted_iota(jnp.int32, (number, number), 1)
    ahead = jnp.where((lax.div(across, per_owner) == down_owner) & (c_at < r_at), 1.0, 0.0)
    slot = down_owner[:, :1].astype(jnp.float32) * float(slots) + jnp.sum(ahead, axis=1, keepdims=True)
    slot_at = lax.broadcasted_iota(jnp.int32, place.shape, 1).astype(jnp.float32)
    spot = slot_at == slot
    line = jnp.max(jnp.where(spot, local_id, 0), axis=0, keepdims=True)
    line = jnp.concatenate([line[:, i * 128:(i + 1) * 128] for i in range(n * slots // 128)], axis=0)
    for d in range(2):
        table[d, me] = line
    place[...] = jnp.where(spot, 1.0, 0.0).astype(place.dtype)
    row_at = lax.broadcasted_iota(jnp.int32, (col, 128), 0) // tok
    lane_at = lax.broadcasted_iota(jnp.int32, (col, 128), 1)
    fold[...] = jnp.where(row_at == lane_at, 1.0, 0.0).astype(fold.dtype)
    for d in range(2):
        table_hop(d, 1, me).start()
    near_table(me).start()
    near_out().start()
    for k in range(1, pieces):
        for d in range(2):
            first(d, k).start()
    to_scalar(0, me, 0).start()

    in_tile = lax.broadcasted_iota(jnp.int32, (tile_rows, feature), 0)
    l_load.wait()
    p_load.wait()

    def fill(i, _):
        for j in range(4):
            p = i * 4 + j
            tile = pas[p].astype(jnp.float32)
            tile = jnp.where(in_tile < len_s[p], tile, tile[0:1, :])
            pas[p] = tile.astype(pas.dtype)
        return 0

    lax.fori_loop(0, per_owner // 4, fill, 0)

    def gather_max(slot, d, b, units_of):
        chosen = [wanted[d, b, my_lane + s] for s in range(cap)]
        for u in units_of:
            qs = qall[b, pl.ds(u * col, col), :]
            near = []
            for s in range(cap):
                sim = lax.dot_general(pas[chosen[s]], qs, (((1,), (1,)), ((), ())),
                                      preferred_element_type=jnp.float32)
                near.append(jnp.max(sim, axis=0, keepdims=True))
            if cap < slots:
                near.append(jnp.zeros((slots - cap, col), jnp.float32))
            near = jnp.concatenate(near, axis=0)
            high = near.astype(jnp.bfloat16).astype(jnp.float32)
            both = jnp.concatenate([high, near - high], axis=0).astype(stage.dtype)
            stage[slot, pl.ds(u * 2 * slots, 2 * slots), :] = both

    def add_up(slot, b):
        part = jnp.dot(stage[slot], fold[...], preferred_element_type=jnp.float32)
        total = None
        for u in range(units):
            at_u = u * 2 * slots
            one = part[at_u:at_u + slots] + part[at_u + slots:at_u + 2 * slots]
            if u > 0:
                one = pltpu.roll(one, u * (col // tok), 1)
            total = one if total is None else total + one
        send_buf[b] = total / float(tok)

    def take_tables(s):
        two_tables(t_recv.at[s - 1]).wait_recv()
        for d in range(2):
            b = origin(d, s, core)

            @pl.when(s < half)
            def _(d=d, b=b):
                table_hop(d, s + 1, b).start()
            table_share(d, s, b).start()
            to_scalar(d, b, 0).start()

    def own_tables(s):
        for d in range(2):
            to_scalar(d, origin(d, s, core), 0).wait()

    def sib_tables(s):
        two_tables(tsib_recv.at[s - 1]).wait_recv()
        for d in range(2):
            to_scalar(d, origin(d, s, 1 - core), 1).start()

    def sib_tables_wait(s):
        for d in range(2):
            to_scalar(d, origin(d, s, 1 - core), 1).wait()

    q_load.wait()
    to_scalar(0, me, 0).wait()
    gather_max(2, 0, me, range(units))
    near_table(sib).wait_recv()
    to_scalar(0, sib, 1).start()
    near_in().wait_recv()
    to_scalar(0, sib, 1).wait()
    gather_max(3, 0, sib, range(units))
    take_tables(1)

    def pair(s, k, c, folds=()):
        base = 0 if c is core else 2
        for slot, b in folds:
            add_up(slot, b)
        for d in range(2):
            gather_max(base + d, d, origin(d, s, c), range(*spans[order[d][k]]))

    def sib_pair(s, k, folds=()):
        if k == 0:
            sib_tables_wait(s)
        so_many(sum(spans[order[d][k]][1] - spans[order[d][k]][0] for d in range(2)),
                sib_recv.at[s - 1, k]).wait_recv()
        pair(s, k, 1 - core, folds)

    def step(s, _):
        opening = s == 1
        old = [jnp.where(opening, me, origin(0, s - 1, 1 - core)),
               jnp.where(opening, sib, origin(1, s - 1, 1 - core))]
        new = [origin(d, s, core) for d in range(2)]
        for k in range(pieces):
            for d in range(2):
                b = new[d]
                hop(d, s, k, b).wait_recv()

                @pl.when(s + 1 < half)
                def _(d=d, k=k, b=b):
                    hop(d, s + 1, k, b).start()
                share(d, s, k, b).start()

            ends = [(d, order[d][k]) for d in range(2)
                    if order[d][k] in (early, late)[d]]
            if ends:
                @pl.when(s + 1 == half)
                def _(ends=ends):
                    for d, p in ends:
                        end_hop(p, new[d]).start()
            if k == 0:
                own_tables(s)
                sib_tables(s)
            if k == pieces - 1:
                take_tables(s + 1)
            pair(s, k, core, [(2, old[0]), (3, old[1])] if k == 0 else ())
            if k == 0:
                score_copy(old[1]).start()

                @pl.when(s > 1)
                def _():
                    score_copy(old[0]).start()
            sib_pair(s, k, [(0, new[0]), (1, new[1])] if k == pieces - 1 else ())
        for b in new:
            score_copy(b).start()
        return 0

    lax.fori_loop(1, half, step, 0)

    mine, other = at(pos + half, core), at(pos + half, 1 - core)
    own_tables(half)
    sib_tables(half)
    groups = [[x[t] for x in (early, late) if t < len(x)] for t in range(max(len(early), len(late)))]
    old = [origin(d, half - 1, 1 - core) for d in range(2)]
    for t, ks in enumerate(groups):
        us = [u for k in ks for u in range(*spans[k])]
        for k in ks:
            end_hop(k, mine).wait_recv()
            end_share(t, k, mine).start()
        if t == 0:
            for d in range(2):
                add_up(2 + d, old[d])
        gather_max(0, 0, mine, us)
        if t == 0:
            for b in old:
                score_copy(b).start()
            sib_tables_wait(half)
        so_many(len(us), tail_recv.at[t]).wait_recv()
        if t == len(groups) - 1:
            add_up(0, mine)
        gather_max(2, 0, other, us)
    score_copy(mine).start()
    add_up(2, other)
    score_copy(other).start()

    remote(qall.at[pl.ds(0, n - 1)], qall.at[pl.ds(0, n - 1)], q_sent.at[0], loc_sem.at[4],
           sib).wait_send()
    remote(table.at[:, pl.ds(0, n // 2)], table.at[:, pl.ds(0, n // 2)], t_sent.at[0],
           loc_sem.at[5], sib).wait_send()
    near_table(me).wait_send()
    all_scores().wait_send()
    all_scores().wait_recv()
    got[me] = send_buf[me]
    spread = None
    for part in split3(got[...].reshape(n * slots, 128)):
        term = jnp.dot(place[...], part, preferred_element_type=jnp.float32)
        spread = term if spread is None else spread + term
    queries = out_ref.shape[0]
    out_ref[...] = spread.T[:queries]
    best_ref[...] = sort_down(spread).T[:queries, :best_ref.shape[1]]


def hand_out(scores_ref, best_ref, scores_hbm, best_hbm, sem):
    moves = [pltpu.make_async_copy(scores_ref, scores_hbm, sem.at[0]),
             pltpu.make_async_copy(best_ref, best_hbm, sem.at[1])]
    for move in moves:
        move.start()
    for move in moves:
        move.wait()


def local(ways, queries, passages, lengths, candidates):
    n = lax.axis_size("corpus")
    per_owner, tile_rows, feature = passages.shape
    per_device, tok = queries.shape[0], queries.shape[1]
    number = candidates.shape[1]
    rows = per_device * tok
    cap = max(2, 3 * number // (2 * n))
    slots = -(-cap // 8) * 8
    col = pick_tile(rows, tok)
    half = n // 4
    units = rows // col
    cfg = (n, ways, cap, per_owner, tile_rows, rows, feature, tok, col)
    dma = pltpu.SemaphoreType.DMA
    scores, best = pl.pallas_call(
        functools.partial(kernel, cfg),
        out_shape=(
            pltpu.VMEM((per_device, number), jnp.float32),
            pltpu.VMEM((per_device, TOPK), jnp.float32),
        ),
        in_specs=[pl.BlockSpec(memory_space=pl.ANY)] * 4,
        out_specs=(
            pl.BlockSpec(memory_space=pltpu.VMEM),
            pl.BlockSpec(memory_space=pltpu.VMEM),
        ),
        scratch_shapes=[
            pltpu.VMEM((n, rows, feature), queries.dtype),
            pltpu.VMEM(passages.shape, passages.dtype),
            pltpu.VMEM((1, number), jnp.int32),
            pltpu.SMEM((per_owner,), jnp.int32),
            pltpu.VMEM((2, n, n * slots // 128, 128), jnp.int32),
            pltpu.SMEM((2, n, 128), jnp.int32),
            pltpu.VMEM((number, n * slots), jnp.bfloat16),
            pltpu.VMEM((col, 128), jnp.bfloat16),
            pltpu.VMEM((4, 2 * slots * units, col), jnp.bfloat16),
            pltpu.VMEM((n, slots, 128), jnp.float32),
            pltpu.VMEM((n, slots, 128), jnp.float32),
            dma((1,)), dma((1,)), dma((1,)),
            dma((2, half - 1, 4)), dma((half - 1, 4)),
            dma((4,)), dma((2,)),
            dma((half,)), dma((half,)),
            dma((1,)),
            dma((2, 2)),
            dma((7,)),
        ],
        compiler_params=pltpu.CompilerParams(
            collective_id=0, has_side_effects=True, vmem_limit_bytes=60 * 2**20),
    )(candidates, lengths, queries.reshape(rows, feature), passages)
    scores = pltpu.with_memory_space_constraint(scores, pltpu.VMEM)
    best = pltpu.with_memory_space_constraint(best, pltpu.VMEM)
    return pl.pallas_call(
        hand_out,
        out_shape=(
            jax.ShapeDtypeStruct((per_device, number), jnp.float32),
            jax.ShapeDtypeStruct((per_device, TOPK), jnp.float32),
        ),
        in_specs=[pl.BlockSpec(memory_space=pltpu.VMEM)] * 2,
        out_specs=(pl.BlockSpec(memory_space=pl.ANY), pl.BlockSpec(memory_space=pl.ANY)),
        scratch_shapes=[dma((2,))],
    )(scores, best)


def solution(mesh):
    ways = 2 if mesh.shape["groups"] == 2 else 1
    return jax.shard_map(
        functools.partial(local, ways),
        mesh=mesh,
        in_specs=(
            P(("groups", "corpus"), None, None),
            P(("groups", "corpus"), None, None),
            P(("groups", "corpus")),
            P(("groups", "corpus"), None),
        ),
        out_specs=(P(("groups", "corpus"), None), P(("groups", "corpus"), None)),
        check_vma=False,
    )
```

```python
import functools

import jax
import jax.numpy as jnp
from jax import lax
from jax.experimental import pallas as pl
from jax.experimental.pallas import tpu as pltpu
from jax.sharding import PartitionSpec as P

TOPK = 100
MESH = pl.DeviceIdType.MESH


def pick_tile(rows, tok):
    tile = 256
    while rows % tile or tile % tok:
        tile //= 2
    return tile


def sort_down(x):
    count, width = x.shape
    index = lax.broadcasted_iota(jnp.int32, (count // 8, 8, width), 0) * 8
    index = index + lax.broadcasted_iota(jnp.int32, (count // 8, 8, width), 1)
    x = x.reshape(count // 8, 8, width)
    size = 2
    while size <= count:
        gap = size // 2
        falling = (index // size) % 2 == 0
        while gap >= 1:
            low = (index // gap) % 2 == 0
            if gap >= 8:
                hop = gap // 8
                y = x.reshape(count // (2 * gap), 2, hop, 8, width)
                y = jnp.concatenate([y[:, 1:], y[:, :1]], axis=1)
                other = y.reshape(x.shape)
            else:
                other = jnp.where(low, pltpu.roll(x, 8 - gap, 1), pltpu.roll(x, gap, 1))
            x = jnp.where(low == falling, jnp.maximum(x, other), jnp.minimum(x, other))
            gap //= 2
        size *= 2
    return x.reshape(count, width)


def split3(x):
    high = x.astype(jnp.bfloat16)
    rest = x - high.astype(jnp.float32)
    mid = rest.astype(jnp.bfloat16)
    low = (rest - mid.astype(jnp.float32)).astype(jnp.bfloat16)
    return high, mid, low


def kernel(cfg, cand_hbm, len_hbm, q_hbm, p_hbm, out_ref, best_ref, qall, pas, cand_v, len_s,
           table, wanted, place, fold, stage, send_buf, got, q_sent, t_sent, sc_sent, q_recv,
           sib_recv, end_recv, tail_recv, t_recv, tsib_recv, sc_recv, sm_sem, loc_sem):
    n, ways, cap, per_owner, tile_rows, rows, feature, tok, col = cfg
    chips = n // 2
    half = chips // 2
    depth = chips // ways
    units = rows // col
    cut = (units + 1) // 2
    first_mid, second_mid = (cut + 1) // 2, (cut + units + 1) // 2
    bits = [(0, first_mid), (first_mid, cut), (cut, second_mid), (second_mid, units)]
    spans = [(0, first_mid), (first_mid, cut), (cut, units)]
    pieces = len(spans)
    order = ((0, 1, 2), (2, 0, 1))
    slots = send_buf.shape[1]
    number = cand_hbm.shape[1]
    me = lax.axis_index("corpus")
    core = lax.rem(me, 2)
    chip = me // 2
    if ways == 2:
        zz, yy = chip // 2, lax.rem(chip, 2)
        pos = (1 - yy) * zz + yy * (2 * depth - 1 - zz)
    else:
        pos = chip

    def at(p, c):
        p = lax.rem(p + 2 * chips, chips)
        if ways == 2:
            far = p // depth
            p = (1 - far) * (2 * p) + far * ((2 * depth - 1 - p) * 2 + 1)
        return p * 2 + c

    sib = at(pos, 1 - core)

    def sign(e, c):
        return 1 - 2 * lax.rem(e + c, 2)

    toward = (at(pos + sign(0, core), core), at(pos + sign(1, core), core))

    def origin(e, s, c):
        return at(pos - sign(e, c) * s, c)

    def remote(src, dst, send, recv, peer):
        return pltpu.make_async_remote_copy(
            src_ref=src, dst_ref=dst, send_sem=send, recv_sem=recv,
            device_id={"corpus": peer}, device_id_type=MESH)

    def span_of(lo, hi):
        return pl.ds(lo * col, (hi - lo) * col)

    def first(d, k):
        cut_k = span_of(*spans[order[d][k]])
        return remote(q_hbm.at[cut_k, :], qall.at[me, cut_k, :],
                      q_sent.at[0], q_recv.at[d, 0, k], toward[d])

    def hop(d, s, k, b):
        piece = qall.at[b, span_of(*spans[order[d][k]]), :]
        return remote(piece, piece, q_sent.at[0], q_recv.at[d, s - 1, k], toward[d])

    def share(d, s, k, b):
        piece = qall.at[b, span_of(*spans[order[d][k]]), :]
        return remote(piece, piece, q_sent.at[0], sib_recv.at[s - 1, k], sib)

    def near_out():
        return remote(q_hbm, qall.at[me], q_sent.at[0], loc_sem.at[4], sib)

    def near_in():
        return remote(qall.at[sib], qall.at[sib], q_sent.at[0], loc_sem.at[4], sib)

    def end_hop(k, b):
        piece = qall.at[b, span_of(*bits[k]), :]
        return remote(piece, piece, q_sent.at[0], end_recv.at[k], toward[k // 2])

    def end_share(t, k, b):
        piece = qall.at[b, span_of(*bits[k]), :]
        return remote(piece, piece, q_sent.at[0], tail_recv.at[t], sib)

    def so_many(count, recv):
        piece = qall.at[0, span_of(0, count), :]
        return remote(piece, piece, q_sent.at[0], recv, sib)

    def table_hop(d, s, b):
        return remote(table.at[d, b], table.at[d, b], t_sent.at[0], t_recv.at[s - 1], toward[d])

    def table_share(d, s, b):
        return remote(table.at[d, b], table.at[d, b], t_sent.at[0], tsib_recv.at[s - 1], sib)

    def two_tables(recv):
        return remote(table.at[:, 0], table.at[:, 0], t_sent.at[0], recv, sib)

    def near_table(b):
        return remote(table.at[0, b], table.at[0, b], loc_sem.at[6], loc_sem.at[5], sib)

    my_row = me * slots // 128
    my_lane = lax.rem(me * slots, 128)

    def to_scalar(d, b, who):
        return pltpu.make_async_copy(table.at[d, b, pl.ds(my_row, 1), :],
                                     wanted.at[d, pl.ds(b, 1), :], sm_sem.at[who, d])

    def score_copy(b):
        return remote(send_buf.at[b], got.at[me], sc_sent.at[0], sc_recv.at[0], b)

    def all_scores():
        return remote(send_buf.at[pl.ds(0, n - 1)], got.at[pl.ds(0, n - 1)],
                      sc_sent.at[0], sc_recv.at[0], sib)

    barrier = pltpu.get_barrier_semaphore()
    for peer in (*toward, sib):
        pl.semaphore_signal(barrier, inc=1, device_id={"corpus": peer}, device_id_type=MESH)
    c_load = pltpu.make_async_copy(cand_hbm, cand_v, loc_sem.at[0])
    q_load = pltpu.make_async_copy(q_hbm, qall.at[me], loc_sem.at[1])
    p_load = pltpu.make_async_copy(p_hbm, pas, loc_sem.at[2])
    l_load = pltpu.make_async_copy(len_hbm, len_s, loc_sem.at[3])
    c_load.start()
    l_load.start()
    pl.semaphore_wait(barrier, 3)
    for d in range(2):
        first(d, 0).start()
    p_load.start()
    q_load.start()

    c_load.wait()
    across = jnp.broadcast_to(cand_v[...], (number, number))
    down = across.T
    down_owner = lax.div(down, per_owner)
    local_id = down[:, :1] - down_owner[:, :1] * per_owner
    r_at = lax.broadcasted_iota(jnp.int32, (number, number), 0)
    c_at = lax.broadcasted_iota(jnp.int32, (number, number), 1)
    ahead = jnp.where((lax.div(across, per_owner) == down_owner) & (c_at < r_at), 1.0, 0.0)
    slot = down_owner[:, :1].astype(jnp.float32) * float(slots) + jnp.sum(ahead, axis=1, keepdims=True)
    slot_at = lax.broadcasted_iota(jnp.int32, place.shape, 1).astype(jnp.float32)
    spot = slot_at == slot
    line = jnp.max(jnp.where(spot, local_id, 0), axis=0, keepdims=True)
    line = jnp.concatenate([line[:, i * 128:(i + 1) * 128] for i in range(n * slots // 128)], axis=0)
    for d in range(2):
        table[d, me] = line
    place[...] = jnp.where(spot, 1.0, 0.0).astype(place.dtype)
    row_at = lax.broadcasted_iota(jnp.int32, (col, 128), 0) // tok
    lane_at = lax.broadcasted_iota(jnp.int32, (col, 128), 1)
    fold[...] = jnp.where(row_at == lane_at, 1.0, 0.0).astype(fold.dtype)
    for d in range(2):
        table_hop(d, 1, me).start()
    near_table(me).start()
    near_out().start()
    for k in range(1, pieces):
        for d in range(2):
            first(d, k).start()
    to_scalar(0, me, 0).start()

    in_tile = lax.broadcasted_iota(jnp.int32, (tile_rows, feature), 0)
    l_load.wait()
    p_load.wait()

    def fill(i, _):
        for j in range(4):
            p = i * 4 + j
            tile = pas[p].astype(jnp.float32)
            tile = jnp.where(in_tile < len_s[p], tile, tile[0:1, :])
            pas[p] = tile.astype(pas.dtype)
        return 0

    lax.fori_loop(0, per_owner // 4, fill, 0)

    def gather_max(slot, d, b, units_of):
        chosen = [wanted[d, b, my_lane + s] for s in range(cap)]
        for u in units_of:
            qs = qall[b, pl.ds(u * col, col), :]
            near = []
            for s in range(cap):
                sim = lax.dot_general(pas[chosen[s]], qs, (((1,), (1,)), ((), ())),
                                      preferred_element_type=jnp.float32)
                near.append(jnp.max(sim, axis=0, keepdims=True))
            if cap < slots:
                near.append(jnp.zeros((slots - cap, col), jnp.float32))
            near = jnp.concatenate(near, axis=0)
            high = near.astype(jnp.bfloat16).astype(jnp.float32)
            both = jnp.concatenate([high, near - high], axis=0).astype(stage.dtype)
            stage[slot, pl.ds(u * 2 * slots, 2 * slots), :] = both

    def add_up(slot, b):
        part = jnp.dot(stage[slot], fold[...], preferred_element_type=jnp.float32)
        total = None
        for u in range(units):
            at_u = u * 2 * slots
            one = part[at_u:at_u + slots] + part[at_u + slots:at_u + 2 * slots]
            if u > 0:
                one = pltpu.roll(one, u * (col // tok), 1)
            total = one if total is None else total + one
        send_buf[b] = total / float(tok)

    def take_tables(s):
        two_tables(t_recv.at[s - 1]).wait_recv()
        for d in range(2):
            b = origin(d, s, core)

            @pl.when(s < half)
            def _(d=d, b=b):
                table_hop(d, s + 1, b).start()
            table_share(d, s, b).start()
            to_scalar(d, b, 0).start()

    def own_tables(s):
        for d in range(2):
            to_scalar(d, origin(d, s, core), 0).wait()

    def sib_tables(s):
        two_tables(tsib_recv.at[s - 1]).wait_recv()
        for d in range(2):
            to_scalar(d, origin(d, s, 1 - core), 1).start()

    def sib_tables_wait(s):
        for d in range(2):
            to_scalar(d, origin(d, s, 1 - core), 1).wait()

    q_load.wait()
    to_scalar(0, me, 0).wait()
    gather_max(2, 0, me, range(units))
    near_table(sib).wait_recv()
    to_scalar(0, sib, 1).start()
    near_in().wait_recv()
    to_scalar(0, sib, 1).wait()
    gather_max(3, 0, sib, range(units))
    take_tables(1)

    def pair(s, k, c, folds=()):
        base = 0 if c is core else 2
        for slot, b in folds:
            add_up(slot, b)
        for d in range(2):
            gather_max(base + d, d, origin(d, s, c), range(*spans[order[d][k]]))

    def sib_pair(s, k, folds=()):
        for slot, b in folds:
            add_up(slot, b)
            score_copy(b).start()
        if k == 0:
            sib_tables_wait(s)
        so_many(sum(spans[order[d][k]][1] - spans[order[d][k]][0] for d in range(2)),
                sib_recv.at[s - 1, k]).wait_recv()
        pair(s, k, 1 - core)

    def step(s, _):
        opening = s == 1
        old = [jnp.where(opening, me, origin(0, s - 1, 1 - core)),
               jnp.where(opening, sib, origin(1, s - 1, 1 - core))]
        new = [origin(d, s, core) for d in range(2)]
        for k in range(pieces):
            for d in range(2):
                b = new[d]
                hop(d, s, k, b).wait_recv()

                @pl.when(s + 1 < half)
                def _(d=d, k=k, b=b):
                    hop(d, s + 1, k, b).start()
                share(d, s, k, b).start()

            ends = [(p, d) for d in range(2) for p in (2 * d, 2 * d + 1)
                    if spans[order[d][k]][0] <= bits[p][0] and bits[p][1] <= spans[order[d][k]][1]]
            if ends:
                @pl.when(s + 1 == half)
                def _(ends=ends):
                    for p, d in ends:
                        end_hop(p, new[d]).start()
            if k == 0:
                own_tables(s)
                sib_tables(s)
            if k == pieces - 1:
                take_tables(s + 1)
            pair(s, k, core, [(2, old[0]), (3, old[1])] if k == 0 else ())
            if k == 0:
                score_copy(old[1]).start()

                @pl.when(s > 1)
                def _():
                    score_copy(old[0]).start()
            sib_pair(s, k, [(0, new[0]), (1, new[1])] if k == pieces - 1 else ())
        return 0

    lax.fori_loop(1, half, step, 0)

    mine, other = at(pos + half, core), at(pos + half, 1 - core)
    own_tables(half)
    sib_tables(half)
    groups = ((0, 2), (1, 3))
    old = [origin(d, half - 1, 1 - core) for d in range(2)]
    for t, ks in enumerate(groups):
        us = [u for k in ks for u in range(*bits[k])]
        for k in ks:
            end_hop(k, mine).wait_recv()
            end_share(t, k, mine).start()
        gather_max(0, 0, mine, us)
        if t == 0:
            for d in range(2):
                add_up(2 + d, old[d])
                score_copy(old[d]).start()
            sib_tables_wait(half)
        if t == len(groups) - 1:
            add_up(0, mine)
            score_copy(mine).start()
        so_many(len(us), tail_recv.at[t]).wait_recv()
        gather_max(2, 0, other, us)
    add_up(2, other)
    score_copy(other).start()

    remote(qall.at[pl.ds(0, n - 1)], qall.at[pl.ds(0, n - 1)], q_sent.at[0], loc_sem.at[4],
           sib).wait_send()
    remote(table.at[:, pl.ds(0, n // 2)], table.at[:, pl.ds(0, n // 2)], t_sent.at[0],
           loc_sem.at[5], sib).wait_send()
    near_table(me).wait_send()
    all_scores().wait_send()
    all_scores().wait_recv()
    got[me] = send_buf[me]
    spread = None
    for part in split3(got[...].reshape(n * slots, 128)):
        term = jnp.dot(place[...], part, preferred_element_type=jnp.float32)
        spread = term if spread is None else spread + term
    queries = out_ref.shape[0]
    out_ref[...] = spread.T[:queries]
    best_ref[...] = sort_down(spread).T[:queries, :best_ref.shape[1]]


def hand_out(scores_ref, best_ref, scores_hbm, best_hbm, sem):
    moves = [pltpu.make_async_copy(scores_ref, scores_hbm, sem.at[0]),
             pltpu.make_async_copy(best_ref, best_hbm, sem.at[1])]
    for move in moves:
        move.start()
    for move in moves:
        move.wait()


def local(ways, queries, passages, lengths, candidates):
    n = lax.axis_size("corpus")
    per_owner, tile_rows, feature = passages.shape
    per_device, tok = queries.shape[0], queries.shape[1]
    number = candidates.shape[1]
    rows = per_device * tok
    cap = max(2, 3 * number // (2 * n))
    slots = -(-cap // 8) * 8
    col = pick_tile(rows, tok)
    half = n // 4
    units = rows // col
    cfg = (n, ways, cap, per_owner, tile_rows, rows, feature, tok, col)
    dma = pltpu.SemaphoreType.DMA
    scores, best = pl.pallas_call(
        functools.partial(kernel, cfg),
        out_shape=(
            pltpu.VMEM((per_device, number), jnp.float32),
            pltpu.VMEM((per_device, TOPK), jnp.float32),
        ),
        in_specs=[pl.BlockSpec(memory_space=pl.ANY)] * 4,
        out_specs=(
            pl.BlockSpec(memory_space=pltpu.VMEM),
            pl.BlockSpec(memory_space=pltpu.VMEM),
        ),
        scratch_shapes=[
            pltpu.VMEM((n, rows, feature), queries.dtype),
            pltpu.VMEM(passages.shape, passages.dtype),
            pltpu.VMEM((1, number), jnp.int32),
            pltpu.SMEM((per_owner,), jnp.int32),
            pltpu.VMEM((2, n, n * slots // 128, 128), jnp.int32),
            pltpu.SMEM((2, n, 128), jnp.int32),
            pltpu.VMEM((number, n * slots), jnp.bfloat16),
            pltpu.VMEM((col, 128), jnp.bfloat16),
            pltpu.VMEM((4, 2 * slots * units, col), jnp.bfloat16),
            pltpu.VMEM((n, slots, 128), jnp.float32),
            pltpu.VMEM((n, slots, 128), jnp.float32),
            dma((1,)), dma((1,)), dma((1,)),
            dma((2, half - 1, 3)), dma((half - 1, 3)),
            dma((4,)), dma((2,)),
            dma((half,)), dma((half,)),
            dma((1,)),
            dma((2, 2)),
            dma((7,)),
        ],
        compiler_params=pltpu.CompilerParams(
            collective_id=0, has_side_effects=True, vmem_limit_bytes=60 * 2**20),
    )(candidates, lengths, queries.reshape(rows, feature), passages)
    scores = pltpu.with_memory_space_constraint(scores, pltpu.VMEM)
    best = pltpu.with_memory_space_constraint(best, pltpu.VMEM)
    return pl.pallas_call(
        hand_out,
        out_shape=(
            jax.ShapeDtypeStruct((per_device, number), jnp.float32),
            jax.ShapeDtypeStruct((per_device, TOPK), jnp.float32),
        ),
        in_specs=[pl.BlockSpec(memory_space=pltpu.VMEM)] * 2,
        out_specs=(pl.BlockSpec(memory_space=pl.ANY), pl.BlockSpec(memory_space=pl.ANY)),
        scratch_shapes=[dma((2,))],
    )(scores, best)


def solution(mesh):
    ways = 2 if mesh.shape["groups"] == 2 else 1
    return jax.shard_map(
        functools.partial(local, ways),
        mesh=mesh,
        in_specs=(
            P(("groups", "corpus"), None, None),
            P(("groups", "corpus"), None, None),
            P(("groups", "corpus")),
            P(("groups", "corpus"), None),
        ),
        out_specs=(P(("groups", "corpus"), None), P(("groups", "corpus"), None)),
        check_vma=False,
    )
```

```python
import functools

import jax
import jax.numpy as jnp
from jax import lax
from jax.experimental import pallas as pl
from jax.experimental.pallas import tpu as pltpu
from jax.sharding import PartitionSpec as P

TOPK = 100
MESH = pl.DeviceIdType.MESH


def pick_tile(rows, tok):
    tile = 256
    while rows % tile or tile % tok:
        tile //= 2
    return tile


def sort_down(x):
    count, width = x.shape
    index = lax.broadcasted_iota(jnp.int32, (count // 8, 8, width), 0) * 8
    index = index + lax.broadcasted_iota(jnp.int32, (count // 8, 8, width), 1)
    x = x.reshape(count // 8, 8, width)
    size = 2
    while size <= count:
        gap = size // 2
        falling = (index // size) % 2 == 0
        while gap >= 1:
            low = (index // gap) % 2 == 0
            if gap >= 8:
                hop = gap // 8
                y = x.reshape(count // (2 * gap), 2, hop, 8, width)
                y = jnp.concatenate([y[:, 1:], y[:, :1]], axis=1)
                other = y.reshape(x.shape)
            else:
                other = jnp.where(low, pltpu.roll(x, 8 - gap, 1), pltpu.roll(x, gap, 1))
            x = jnp.where(low == falling, jnp.maximum(x, other), jnp.minimum(x, other))
            gap //= 2
        size *= 2
    return x.reshape(count, width)


def split3(x):
    high = x.astype(jnp.bfloat16)
    rest = x - high.astype(jnp.float32)
    mid = rest.astype(jnp.bfloat16)
    low = (rest - mid.astype(jnp.float32)).astype(jnp.bfloat16)
    return high, mid, low


def kernel(cfg, cand_hbm, len_hbm, q_hbm, p_hbm, out_ref, best_ref, qall, pas, cand_v, len_s,
           table, wanted, place, fold, stage, send_buf, got, q_sent, t_sent, sc_sent, q_recv,
           sib_recv, end_recv, tail_recv, t_recv, tsib_recv, sc_recv, sm_sem, loc_sem):
    n, ways, cap, per_owner, tile_rows, rows, feature, tok, col = cfg
    chips = n // 2
    half = chips // 2
    depth = chips // ways
    units = rows // col
    cut = (units + 1) // 2
    first_mid, second_mid = (cut + 1) // 2, (cut + units + 1) // 2
    bits = [(0, first_mid), (first_mid, cut), (cut, second_mid), (second_mid, units)]
    spans = [(0, first_mid), (first_mid, cut), (cut, units)]
    pieces = len(spans)
    order = ((0, 1, 2), (2, 0, 1))
    slots = send_buf.shape[1]
    number = cand_hbm.shape[1]
    me = lax.axis_index("corpus")
    core = lax.rem(me, 2)
    chip = me // 2
    if ways == 2:
        zz, yy = chip // 2, lax.rem(chip, 2)
        pos = (1 - yy) * zz + yy * (2 * depth - 1 - zz)
    else:
        pos = chip

    def at(p, c):
        p = lax.rem(p + 2 * chips, chips)
        if ways == 2:
            far = p // depth
            p = (1 - far) * (2 * p) + far * ((2 * depth - 1 - p) * 2 + 1)
        return p * 2 + c

    sib = at(pos, 1 - core)

    def sign(e, c):
        return 1 - 2 * lax.rem(e + c, 2)

    toward = (at(pos + sign(0, core), core), at(pos + sign(1, core), core))

    def origin(e, s, c):
        return at(pos - sign(e, c) * s, c)

    def remote(src, dst, send, recv, peer):
        return pltpu.make_async_remote_copy(
            src_ref=src, dst_ref=dst, send_sem=send, recv_sem=recv,
            device_id={"corpus": peer}, device_id_type=MESH)

    def span_of(lo, hi):
        return pl.ds(lo * col, (hi - lo) * col)

    def first(d, k):
        cut_k = span_of(*spans[order[d][k]])
        return remote(qall.at[me, cut_k, :], qall.at[me, cut_k, :],
                      q_sent.at[0], q_recv.at[d, 0, k], toward[d])

    def hop(d, s, k, b):
        piece = qall.at[b, span_of(*spans[order[d][k]]), :]
        return remote(piece, piece, q_sent.at[0], q_recv.at[d, s - 1, k], toward[d])

    def share(d, s, k, b):
        piece = qall.at[b, span_of(*spans[order[d][k]]), :]
        return remote(piece, piece, q_sent.at[0], sib_recv.at[s - 1, k], sib)

    def near_out():
        return remote(qall.at[me], qall.at[me], q_sent.at[0], loc_sem.at[4], sib)

    def near_in():
        return remote(qall.at[sib], qall.at[sib], q_sent.at[0], loc_sem.at[4], sib)

    def end_hop(k, b):
        piece = qall.at[b, span_of(*bits[k]), :]
        return remote(piece, piece, q_sent.at[0], end_recv.at[k], toward[k // 2])

    def end_share(t, k, b):
        piece = qall.at[b, span_of(*bits[k]), :]
        return remote(piece, piece, q_sent.at[0], tail_recv.at[t], sib)

    def so_many(count, recv):
        piece = qall.at[0, span_of(0, count), :]
        return remote(piece, piece, q_sent.at[0], recv, sib)

    def table_hop(d, s, b):
        return remote(table.at[d, b], table.at[d, b], t_sent.at[0], t_recv.at[s - 1], toward[d])

    def table_share(d, s, b):
        return remote(table.at[d, b], table.at[d, b], t_sent.at[0], tsib_recv.at[s - 1], sib)

    def two_tables(recv):
        return remote(table.at[:, 0], table.at[:, 0], t_sent.at[0], recv, sib)

    def near_table(b):
        return remote(table.at[0, b], table.at[0, b], loc_sem.at[6], loc_sem.at[5], sib)

    my_row = me * slots // 128
    my_lane = lax.rem(me * slots, 128)

    def to_scalar(d, b, who):
        return pltpu.make_async_copy(table.at[d, b, pl.ds(my_row, 1), :],
                                     wanted.at[d, pl.ds(b, 1), :], sm_sem.at[who, d])

    def score_copy(b):
        return remote(send_buf.at[b], got.at[me], sc_sent.at[0], sc_recv.at[0], b)

    def all_scores():
        return remote(send_buf.at[pl.ds(0, n - 1)], got.at[pl.ds(0, n - 1)],
                      sc_sent.at[0], sc_recv.at[0], sib)

    barrier = pltpu.get_barrier_semaphore()
    for peer in (*toward, sib):
        pl.semaphore_signal(barrier, inc=1, device_id={"corpus": peer}, device_id_type=MESH)
    c_load = pltpu.make_async_copy(cand_hbm, cand_v, loc_sem.at[0])
    q_load = pltpu.make_async_copy(q_hbm, qall.at[me], loc_sem.at[1])
    p_load = pltpu.make_async_copy(p_hbm, pas, loc_sem.at[2])
    l_load = pltpu.make_async_copy(len_hbm, len_s, loc_sem.at[3])
    c_load.start()
    l_load.start()
    q_load.start()
    pl.semaphore_wait(barrier, 3)
    q_load.wait()
    for d in range(2):
        first(d, 0).start()
    p_load.start()

    c_load.wait()
    across = jnp.broadcast_to(cand_v[...], (number, number))
    down = across.T
    down_owner = lax.div(down, per_owner)
    local_id = down[:, :1] - down_owner[:, :1] * per_owner
    r_at = lax.broadcasted_iota(jnp.int32, (number, number), 0)
    c_at = lax.broadcasted_iota(jnp.int32, (number, number), 1)
    ahead = jnp.where((lax.div(across, per_owner) == down_owner) & (c_at < r_at), 1.0, 0.0)
    slot = down_owner[:, :1].astype(jnp.float32) * float(slots) + jnp.sum(ahead, axis=1, keepdims=True)
    slot_at = lax.broadcasted_iota(jnp.int32, place.shape, 1).astype(jnp.float32)
    spot = slot_at == slot
    line = jnp.max(jnp.where(spot, local_id, 0), axis=0, keepdims=True)
    line = jnp.concatenate([line[:, i * 128:(i + 1) * 128] for i in range(n * slots // 128)], axis=0)
    for d in range(2):
        table[d, me] = line
    place[...] = jnp.where(spot, 1.0, 0.0).astype(place.dtype)
    row_at = lax.broadcasted_iota(jnp.int32, (col, 128), 0) // tok
    lane_at = lax.broadcasted_iota(jnp.int32, (col, 128), 1)
    fold[...] = jnp.where(row_at == lane_at, 1.0, 0.0).astype(fold.dtype)
    for d in range(2):
        table_hop(d, 1, me).start()
    near_table(me).start()
    near_out().start()
    for k in range(1, pieces):
        for d in range(2):
            first(d, k).start()
    to_scalar(0, me, 0).start()

    in_tile = lax.broadcasted_iota(jnp.int32, (tile_rows, feature), 0)
    l_load.wait()
    p_load.wait()

    def fill(i, _):
        for j in range(4):
            p = i * 4 + j
            tile = pas[p].astype(jnp.float32)
            tile = jnp.where(in_tile < len_s[p], tile, tile[0:1, :])
            pas[p] = tile.astype(pas.dtype)
        return 0

    lax.fori_loop(0, per_owner // 4, fill, 0)

    def gather_max(slot, d, b, units_of):
        chosen = [wanted[d, b, my_lane + s] for s in range(cap)]
        for u in units_of:
            qs = qall[b, pl.ds(u * col, col), :]
            near = []
            for s in range(cap):
                sim = lax.dot_general(pas[chosen[s]], qs, (((1,), (1,)), ((), ())),
                                      preferred_element_type=jnp.float32)
                near.append(jnp.max(sim, axis=0, keepdims=True))
            if cap < slots:
                near.append(jnp.zeros((slots - cap, col), jnp.float32))
            near = jnp.concatenate(near, axis=0)
            high = near.astype(jnp.bfloat16).astype(jnp.float32)
            both = jnp.concatenate([high, near - high], axis=0).astype(stage.dtype)
            stage[slot, pl.ds(u * 2 * slots, 2 * slots), :] = both

    def add_up(slot, b):
        part = jnp.dot(stage[slot], fold[...], preferred_element_type=jnp.float32)
        total = None
        for u in range(units):
            at_u = u * 2 * slots
            one = part[at_u:at_u + slots] + part[at_u + slots:at_u + 2 * slots]
            if u > 0:
                one = pltpu.roll(one, u * (col // tok), 1)
            total = one if total is None else total + one
        send_buf[b] = total / float(tok)

    def take_tables(s):
        two_tables(t_recv.at[s - 1]).wait_recv()
        for d in range(2):
            b = origin(d, s, core)

            @pl.when(s < half)
            def _(d=d, b=b):
                table_hop(d, s + 1, b).start()
            table_share(d, s, b).start()
            to_scalar(d, b, 0).start()

    def own_tables(s):
        for d in range(2):
            to_scalar(d, origin(d, s, core), 0).wait()

    def sib_tables(s):
        two_tables(tsib_recv.at[s - 1]).wait_recv()
        for d in range(2):
            to_scalar(d, origin(d, s, 1 - core), 1).start()

    def sib_tables_wait(s):
        for d in range(2):
            to_scalar(d, origin(d, s, 1 - core), 1).wait()

    to_scalar(0, me, 0).wait()
    gather_max(2, 0, me, range(units))
    near_table(sib).wait_recv()
    to_scalar(0, sib, 1).start()
    near_in().wait_recv()
    to_scalar(0, sib, 1).wait()
    gather_max(3, 0, sib, range(units))
    take_tables(1)

    def pair(s, k, c, folds=()):
        base = 0 if c is core else 2
        for slot, b in folds:
            add_up(slot, b)
        for d in range(2):
            gather_max(base + d, d, origin(d, s, c), range(*spans[order[d][k]]))

    def sib_pair(s, k, folds=()):
        for slot, b in folds:
            add_up(slot, b)
            score_copy(b).start()
        if k == 0:
            sib_tables_wait(s)
        so_many(sum(spans[order[d][k]][1] - spans[order[d][k]][0] for d in range(2)),
                sib_recv.at[s - 1, k]).wait_recv()
        pair(s, k, 1 - core)

    def step(s, _):
        opening = s == 1
        old = [jnp.where(opening, me, origin(0, s - 1, 1 - core)),
               jnp.where(opening, sib, origin(1, s - 1, 1 - core))]
        new = [origin(d, s, core) for d in range(2)]
        for k in range(pieces):
            for d in range(2):
                b = new[d]
                hop(d, s, k, b).wait_recv()

                @pl.when(s + 1 < half)
                def _(d=d, k=k, b=b):
                    hop(d, s + 1, k, b).start()
                share(d, s, k, b).start()

            ends = [(p, d) for d in range(2) for p in (2 * d, 2 * d + 1)
                    if spans[order[d][k]][0] <= bits[p][0] and bits[p][1] <= spans[order[d][k]][1]]
            if ends:
                @pl.when(s + 1 == half)
                def _(ends=ends):
                    for p, d in ends:
                        end_hop(p, new[d]).start()
            if k == 0:
                own_tables(s)
                sib_tables(s)
            if k == pieces - 1:
                take_tables(s + 1)
            pair(s, k, core, [(2, old[0]), (3, old[1])] if k == 0 else ())
            if k == 0:
                score_copy(old[1]).start()

                @pl.when(s > 1)
                def _():
                    score_copy(old[0]).start()
            sib_pair(s, k, [(0, new[0]), (1, new[1])] if k == pieces - 1 else ())
        return 0

    lax.fori_loop(1, half, step, 0)

    mine, other = at(pos + half, core), at(pos + half, 1 - core)
    own_tables(half)
    sib_tables(half)
    groups = ((0, 2), (1, 3))
    old = [origin(d, half - 1, 1 - core) for d in range(2)]
    for t, ks in enumerate(groups):
        us = [u for k in ks for u in range(*bits[k])]
        for k in ks:
            end_hop(k, mine).wait_recv()
            end_share(t, k, mine).start()
        gather_max(0, 0, mine, us)
        if t == 0:
            for d in range(2):
                add_up(2 + d, old[d])
                score_copy(old[d]).start()
            sib_tables_wait(half)
        if t == len(groups) - 1:
            add_up(0, mine)
            score_copy(mine).start()
        so_many(len(us), tail_recv.at[t]).wait_recv()
        gather_max(2, 0, other, us)
    add_up(2, other)
    score_copy(other).start()

    remote(qall.at[pl.ds(0, n - 1)], qall.at[pl.ds(0, n - 1)], q_sent.at[0], loc_sem.at[4],
           sib).wait_send()
    remote(table.at[:, pl.ds(0, n // 2)], table.at[:, pl.ds(0, n // 2)], t_sent.at[0],
           loc_sem.at[5], sib).wait_send()
    near_table(me).wait_send()
    all_scores().wait_send()
    all_scores().wait_recv()
    got[me] = send_buf[me]
    spread = None
    for part in split3(got[...].reshape(n * slots, 128)):
        term = jnp.dot(place[...], part, preferred_element_type=jnp.float32)
        spread = term if spread is None else spread + term
    queries = out_ref.shape[0]
    out_ref[...] = spread.T[:queries]
    best_ref[...] = sort_down(spread).T[:queries, :best_ref.shape[1]]


def hand_out(scores_ref, best_ref, scores_hbm, best_hbm, sem):
    moves = [pltpu.make_async_copy(scores_ref, scores_hbm, sem.at[0]),
             pltpu.make_async_copy(best_ref, best_hbm, sem.at[1])]
    for move in moves:
        move.start()
    for move in moves:
        move.wait()


def local(ways, queries, passages, lengths, candidates):
    n = lax.axis_size("corpus")
    per_owner, tile_rows, feature = passages.shape
    per_device, tok = queries.shape[0], queries.shape[1]
    number = candidates.shape[1]
    rows = per_device * tok
    cap = max(2, 3 * number // (2 * n))
    slots = -(-cap // 8) * 8
    col = pick_tile(rows, tok)
    half = n // 4
    units = rows // col
    cfg = (n, ways, cap, per_owner, tile_rows, rows, feature, tok, col)
    dma = pltpu.SemaphoreType.DMA
    scores, best = pl.pallas_call(
        functools.partial(kernel, cfg),
        out_shape=(
            pltpu.VMEM((per_device, number), jnp.float32),
            pltpu.VMEM((per_device, TOPK), jnp.float32),
        ),
        in_specs=[pl.BlockSpec(memory_space=pl.ANY)] * 4,
        out_specs=(
            pl.BlockSpec(memory_space=pltpu.VMEM),
            pl.BlockSpec(memory_space=pltpu.VMEM),
        ),
        scratch_shapes=[
            pltpu.VMEM((n, rows, feature), queries.dtype),
            pltpu.VMEM(passages.shape, passages.dtype),
            pltpu.VMEM((1, number), jnp.int32),
            pltpu.SMEM((per_owner,), jnp.int32),
            pltpu.VMEM((2, n, n * slots // 128, 128), jnp.int32),
            pltpu.SMEM((2, n, 128), jnp.int32),
            pltpu.VMEM((number, n * slots), jnp.bfloat16),
            pltpu.VMEM((col, 128), jnp.bfloat16),
            pltpu.VMEM((4, 2 * slots * units, col), jnp.bfloat16),
            pltpu.VMEM((n, slots, 128), jnp.float32),
            pltpu.VMEM((n, slots, 128), jnp.float32),
            dma((1,)), dma((1,)), dma((1,)),
            dma((2, half - 1, 3)), dma((half - 1, 3)),
            dma((4,)), dma((2,)),
            dma((half,)), dma((half,)),
            dma((1,)),
            dma((2, 2)),
            dma((7,)),
        ],
        compiler_params=pltpu.CompilerParams(
            collective_id=0, has_side_effects=True, vmem_limit_bytes=60 * 2**20),
    )(candidates, lengths, queries.reshape(rows, feature), passages)
    scores = pltpu.with_memory_space_constraint(scores, pltpu.VMEM)
    best = pltpu.with_memory_space_constraint(best, pltpu.VMEM)
    return pl.pallas_call(
        hand_out,
        out_shape=(
            jax.ShapeDtypeStruct((per_device, number), jnp.float32),
            jax.ShapeDtypeStruct((per_device, TOPK), jnp.float32),
        ),
        in_specs=[pl.BlockSpec(memory_space=pltpu.VMEM)] * 2,
        out_specs=(pl.BlockSpec(memory_space=pl.ANY), pl.BlockSpec(memory_space=pl.ANY)),
        scratch_shapes=[dma((2,))],
    )(scores, best)


def solution(mesh):
    ways = 2 if mesh.shape["groups"] == 2 else 1
    return jax.shard_map(
        functools.partial(local, ways),
        mesh=mesh,
        in_specs=(
            P(("groups", "corpus"), None, None),
            P(("groups", "corpus"), None, None),
            P(("groups", "corpus")),
            P(("groups", "corpus"), None),
        ),
        out_specs=(P(("groups", "corpus"), None), P(("groups", "corpus"), None)),
        check_vma=False,
    )
```
